256 devices in a mesh: rep: 32 (over z, x_hi, core), exp: 8 (over x_lo, y).
Axes of the slice: x: 4 (x_hi: 2, x_lo: 2; x = x_hi * 2 + x_lo), y: 4, z: 8, core: 2. Of those that a mesh axis runs over, the one named last changes fastest.
Arguments:
- residual: bfloat16 [3, 512, 4096], P(None, ('rep', 'exp')), may hold values from -6 to 6
- queries: bfloat16 [3, 512, 4096], P(None, ('rep', 'exp')), may hold values from -30 to 30
- key_cache: bfloat16 [512, 1024, 256], P(('rep', 'exp')), may hold values from -6 to 6
- value_cache: bfloat16 [512, 1024, 256], P(('rep', 'exp')), may hold values from -6 to 6
- new_keys: bfloat16 [3, 512, 256], P(None, ('rep', 'exp')), may hold values from -6 to 6
- new_values: bfloat16 [3, 512, 256], P(None, ('rep', 'exp')), may hold values from -6 to 6
- cache_len: int32 [512], P(('rep', 'exp')), may hold values from 128 to 1024, as said below
- norm_gain: bfloat16 [4096], replicated, may hold values from 0.099609375 to 1.8984375
- expert_ids: int32 [3, 512, 8], P(None, ('rep', 'exp')), may hold values from 0 to 63, all different within a row; in each aligned block of 16 rows (0 to 15, 16 to 31, ..., all dimensions but the last counted through in order) at most 4 rows name the same one
- gate_scores: int32 [3, 512, 8], P(None, ('rep', 'exp')), may hold values from 1 to 1000
- gate_weight: bfloat16 [64, 1536, 4096], P('rep', 'exp'), may hold values from -0.09375 to 0.09375
- up_weight: bfloat16 [64, 1536, 4096], P('rep', 'exp'), may hold values from -0.09375 to 0.09375
- down_weight: bfloat16 [64, 1536, 4096], P('rep', 'exp'), may hold values from -0.15625 to 0.15625
Outputs:
- mixed: bfloat16 [3, 512, 4096], P(None, ('rep', 'exp'))
The draws below stay inside these ranges and needn't reach their ends.
Inputs may be any that keep to these rules, and one draw needn't show every extreme that they name: `expert_ids`: within each step and each aligned block of 16 sequences (the sequences of one index of rep), no expert is named more than 4 times, and that count is reached; a token names different experts. `cache_len`: some sequence holds all 1024 cached tokens.
All inputs are finite; a program needn't handle non-finite values.
Results may differ from the reference program's by a relative error of at most 0.013.
Values may be sent and summed in bfloat16 or wider, within the bound.
No kernel may reach another device: no remote copies, remote signals or barrier semaphores. Data moves between devices by JAX's collectives and lax.ppermute only.
A program may use at most 128 MiB of HBM per device.

```python
import math
import jax
import jax.numpy as jnp
import numpy as np
from jax import lax

D = 4096
FF = 1536
HD = 128
QH = 32
KVH = 2
TOPK = 8
CAPE = 4
STEPS = 3
SEQ_DEV = 2
CACHE = 1024
BATCH = 512
EXPERTS = 64
N_REP = 32
N_EXP = 8


def draw_queries(key, part):
    drawn = jnp.clip(jax.random.normal(jax.random.fold_in(key, 31), (STEPS, BATCH, QH * HD), jnp.float32), -6.0, 6.0)
    return drawn.astype(jnp.bfloat16)


def draw_key_cache(key, part):
    drawn = jnp.clip(jax.random.normal(jax.random.fold_in(key, 11), (BATCH, CACHE, KVH * HD), jnp.float32), -6.0, 6.0)
    return drawn.astype(jnp.bfloat16)


def draw_cache_len(key, part):
    cache_lengths = jax.random.randint(jax.random.fold_in(key, 21), (BATCH,), CACHE // 8, CACHE + 1)
    longest = jax.random.randint(jax.random.fold_in(key, 22), (), 0, BATCH)
    return cache_lengths.at[longest].set(CACHE)


def set_ends(drawn, key, low, top_value):
    longest = drawn.shape.index(max(drawn.shape))
    spots = []
    for shift in (0, 1):
        where = [jax.random.randint(jax.random.fold_in(key, axis), (), 0, length) for axis, length in enumerate(drawn.shape)]
        where[longest] = (where[longest] + shift) % drawn.shape[longest]
        spots.append(tuple(where))
    return drawn.at[spots[0]].set(low).at[spots[1]].set(top_value)


def block_levels(own_key, shape, shards, least, top_value):
    level, own = 1.0, jax.random.fold_in(own_key, 6)
    for dim, parts in shards:
        draws = jnp.exp(jax.random.uniform(jax.random.fold_in(own, dim), (parts,), jnp.float32, least / len(shards), top_value / len(shards)))
        level = level * jnp.repeat(draws, shape[dim] // parts).reshape([-1 if axis == dim else 1 for axis in range(len(shape))])
    return level


def assign_block(stream_key, own, number, rows, amount, top, reach, skew):
    order = jax.random.permutation(stream_key, amount)
    crowded, usual = shares(amount, rows * top, reach, skew, True), shares(amount, rows * top, reach, skew, False)
    places = jnp.arange(amount)

    def named(lengths, rotation):
        used = int((lengths > 0).sum())
        fixed = max(1, used // 4)
        shifted = fixed + (places - fixed + rotation * (used - fixed)) % max(1, amount - fixed)
        return jnp.zeros((amount,), jnp.int32).at[order[jnp.where(places < fixed, places, shifted)]].set(jnp.asarray(lengths, jnp.int32))

    lengths = jnp.where(number % 4 == 0, named(crowded, number // 4), named(usual, number - number // 4 - 1))
    mixed = jax.random.permutation(jax.random.fold_in(own, 3), amount)
    giver, sink = mixed[0:amount // 2 * 2:2], mixed[1:amount // 2 * 2:2]
    slack = jnp.minimum(lengths[giver] - 1, reach - lengths[sink]) // 2
    slack = jnp.where((giver == order[0]) | (sink == order[0]) | (lengths[sink] == 0), 0, jnp.maximum(slack, 0))
    shifted = jax.random.randint(jax.random.fold_in(own, 4), (amount // 2,), 0, 1 << 20) % (slack + 1)
    lengths = lengths.at[giver].add(-shifted).at[sink].add(shifted)
    labels = jnp.searchsorted(jnp.cumsum(lengths), jnp.arange(rows * top), side="right").astype(jnp.int32)
    grid = labels.reshape(top, rows).T
    grid = grid[jax.random.permutation(jax.random.fold_in(own, 1), rows)]
    rotation = jax.random.randint(jax.random.fold_in(own, 2), (rows, 1), 0, top)
    return jnp.take_along_axis(grid, (jnp.arange(top)[None, :] + rotation) % top, axis=1)


def shares(count, total, bound, skew, full):
    loads = [(1 << 20) // math.isqrt(grade ** skew) + 1 for grade in range(1, count + 1)]
    largest = bound if full else min(bound, max(-(-total // count), total * loads[0] // sum(loads)))
    least = 1 if total - largest >= count - 1 else 0
    holding, rest = [largest] + [least] * (count - 1), total - largest - least * (count - 1)
    while rest > 0:
        candidates = [i for i in range(1, count) if holding[i] < largest] or [i for i in range(1, count) if holding[i] < bound]
        mass, budget = sum([loads[i] for i in candidates]), rest
        for i in candidates:
            extra = min(bound - holding[i], max(1, budget * loads[i] // mass), rest)
            holding[i] = holding[i] + extra
            rest = rest - extra
    return np.array(holding)


def scatter_about(rng, extent, deviation, reach, pieces=(), kind=jnp.bfloat16):
    drawn = deviation * jax.random.normal(rng, extent, jnp.float32)
    if pieces:
        drawn = drawn * block_levels(rng, extent, pieces, -0.22, 0.18)
    return jnp.clip(drawn, -reach, reach).astype(kind)


def setup_inputs(seed: int = 0) -> dict:
    arg_keys = jax.random.split(jax.random.key(seed), 14)
    residual = scatter_about(arg_keys[0], (STEPS, BATCH, D), 0.5, 6.0, ((1, 256),))
    queries = draw_queries(jax.random.fold_in(arg_keys[13], 71), 0)
    key_cache = draw_key_cache(jax.random.fold_in(arg_keys[13], 71), 0)
    value_cache = scatter_about(arg_keys[3], (BATCH, CACHE, KVH * HD), 1.0, 6.0, ((0, 256),))
    new_keys = scatter_about(arg_keys[4], (STEPS, BATCH, KVH * HD), 1.0, 6.0, ((1, 256),))
    new_values = scatter_about(arg_keys[5], (STEPS, BATCH, KVH * HD), 1.0, 6.0, ((1, 256),))
    cache_len = draw_cache_len(jax.random.fold_in(arg_keys[13], 71), 0)
    norm_gain = jnp.clip(1.0 + 0.18 * jax.random.normal(arg_keys[7], (D,), jnp.float32), 0.099609375, 1.8984375).astype(jnp.bfloat16)
    expert_ids_keys = jax.random.split(jax.random.fold_in(arg_keys[8], 1), STEPS * BATCH // (N_EXP * SEQ_DEV))
    expert_ids_turns = jax.random.permutation(jax.random.fold_in(arg_keys[8], 3), STEPS * BATCH // (N_EXP * SEQ_DEV))
    expert_ids = jax.vmap(lambda own, number: assign_block(jax.random.fold_in(arg_keys[8], 2), own, number, N_EXP * SEQ_DEV, EXPERTS, TOPK, CAPE, 2))(expert_ids_keys, expert_ids_turns).reshape((STEPS, BATCH, TOPK))
    gate_scores = set_ends(jax.random.randint(arg_keys[9], (STEPS, BATCH, TOPK), 1, 1001), jax.random.fold_in(arg_keys[9], 1), 1, 1000).astype(jnp.int32)
    gate_weight = scatter_about(arg_keys[10], (EXPERTS, FF, D), D ** -0.5, 0.09375, ((0, 32), (1, 8)))
    up_weight = scatter_about(arg_keys[11], (EXPERTS, FF, D), D ** -0.5, 0.09375, ((0, 32), (1, 8)))
    down_weight = scatter_about(arg_keys[12], (EXPERTS, FF, D), FF ** -0.5, 0.15625, ((0, 32), (1, 8)))
    return dict(residual=residual, queries=queries, key_cache=key_cache, value_cache=value_cache, new_keys=new_keys, new_values=new_values, cache_len=cache_len, norm_gain=norm_gain, expert_ids=expert_ids, gate_scores=gate_scores, gate_weight=gate_weight, up_weight=up_weight, down_weight=down_weight)


def attend_row(operands, step):
    head_query, keys_old, values_old, keys_new, values_new, length = operands
    group_size = QH // KVH
    scaling = 1.0 / math.sqrt(HD)
    joined_key_rows = jnp.concatenate([keys_old, keys_new], axis=0).astype(jnp.float32).reshape(CACHE + STEPS, KVH, HD)
    all_values = jnp.concatenate([values_old, values_new], axis=0).astype(jnp.float32).reshape(CACHE + STEPS, KVH, HD)
    query_heads = head_query.astype(jnp.float32).reshape(KVH, group_size, HD)
    scores = jnp.einsum('jgd,tjd->jgt', query_heads, joined_key_rows) * scaling
    position = jnp.arange(CACHE + STEPS, dtype=jnp.int32)
    valid = jnp.where(position < CACHE, position < length, position - CACHE <= step)
    scores = jnp.where(valid[None, None, :], scores, -1e+30)
    row_max = lax.optimization_barrier(jnp.max(scores, axis=-1, keepdims=True))
    expo = jnp.exp(scores - row_max)
    probs = (expo / lax.optimization_barrier(jnp.sum(expo, axis=-1, keepdims=True))).astype(jnp.bfloat16)
    blended = jnp.einsum('jgt,tjd->jgd', probs.astype(jnp.float32), all_values)
    return blended.reshape(QH * HD)

def norm_rows(hidden, norm_gain):
    mean_square = lax.optimization_barrier(jnp.mean(hidden * hidden, axis=-1, keepdims=True))
    return (hidden * lax.rsqrt(mean_square + 1e-06) * norm_gain.astype(jnp.float32)).astype(jnp.bfloat16)

def slot_targets(chosen, experts):
    flat_ids = chosen.reshape(-1)
    matches = (flat_ids[:, None] == jnp.arange(experts, dtype=jnp.int32)[None, :]).astype(jnp.int32)
    ranking = jnp.cumsum(matches, axis=0) - 1
    slot_rank = lax.optimization_barrier(jnp.sum(matches * ranking, axis=1))
    return (flat_ids * CAPE + slot_rank).reshape(chosen.shape)

def run_expert(operands, normed):
    row_index, gate_w, up_w, down_w = operands
    picked_rows = jnp.where((row_index > 0)[:, None], normed[jnp.maximum(row_index - 1, 0)], jnp.zeros((), jnp.bfloat16))
    gate_act = jnp.dot(picked_rows, gate_w.T, preferred_element_type=jnp.float32)
    up_act = jnp.dot(picked_rows, up_w.T, preferred_element_type=jnp.float32)
    hidden_activation = (jax.nn.silu(gate_act) * up_act).astype(jnp.bfloat16)
    unit_groups = hidden_activation.reshape(-1, N_EXP, FF // N_EXP).astype(jnp.float32)
    down_groups = down_w.reshape(N_EXP, FF // N_EXP, D).astype(jnp.float32)
    partial_value = jnp.einsum('rnf,nfd->rnd', unit_groups, down_groups)
    partial_value = lax.optimization_barrier(partial_value.astype(jnp.bfloat16)).astype(jnp.float32)
    return lax.optimization_barrier(jnp.sum(partial_value, axis=1))

def expert_mix(normed, chosen, gate_values, gate_weight, up_weight, down_weight):
    group_rows = N_EXP * SEQ_DEV
    grouped = chosen.reshape(N_REP, group_rows, TOPK)
    target = jax.vmap(lambda piece: slot_targets(piece, EXPERTS))(grouped)
    group_of = jnp.arange(N_REP, dtype=jnp.int32)[:, None, None]
    expert_of = target // CAPE
    slot_of = target % CAPE
    position_flat = (expert_of * N_REP + group_of) * CAPE + slot_of
    row_of = jnp.broadcast_to(jnp.arange(BATCH, dtype=jnp.int32).reshape(N_REP, group_rows, 1), position_flat.shape)
    table = jnp.zeros((EXPERTS * N_REP * CAPE,), jnp.int32).at[position_flat.reshape(-1)].set(row_of.reshape(-1) + 1)
    table = table.reshape(EXPERTS, N_REP * CAPE)
    outputs = lax.map(lambda operands: run_expert(operands, normed), (table, gate_weight, up_weight, down_weight))
    outputs = outputs.reshape(EXPERTS * N_REP * CAPE, D)
    selected_experts = jnp.take(outputs, position_flat.reshape(BATCH, TOPK), axis=0)
    return jnp.einsum('sv,svr->sr', gate_values, selected_experts)

def reference(residual, queries, key_cache, value_cache, new_keys, new_values, cache_len, norm_gain, expert_ids, gate_scores, gate_weight, up_weight, down_weight):
    keys_by_row = jnp.swapaxes(new_keys, 0, 1)
    values_by_row = jnp.swapaxes(new_values, 0, 1)
    results = []
    for step in range(STEPS):
        attention = lax.map(lambda operands: attend_row(operands, step), (queries[step], key_cache, value_cache, keys_by_row, values_by_row, cache_len))
        hidden = residual[step].astype(jnp.float32) + attention
        normed = norm_rows(hidden, norm_gain)
        unscaled_scores = gate_scores[step].astype(jnp.float32)
        gate_values = unscaled_scores / lax.optimization_barrier(jnp.sum(unscaled_scores, axis=-1, keepdims=True))
        expert_sum = expert_mix(normed, expert_ids[step], gate_values, gate_weight, up_weight, down_weight)
        results.append((hidden + expert_sum).astype(jnp.bfloat16))
    return jnp.stack(results)
```

```python
import math

import numpy as np

import jax
import jax.numpy as jnp
from jax import lax
from jax.sharding import PartitionSpec as P

D = 4096
FF = 1536
HD = 128
QH = 32
KVH = 2
TOPK = 8
CAPE = 4
STEPS = 3
CACHE = 1024
N_EXP = 8
SEQ = 2
UNITS = FF // N_EXP
TOK = N_EXP * STEPS * SEQ
BLK = D // 4
THIRD = UNITS // 3

PARITY = [(e // 4 + e % 4) % 2 for e in range(N_EXP)]
GROUPS = [[e for e in range(N_EXP) if PARITY[e] == side] for side in range(2)]
NEAR = [4, 1, 3]
SAME = [0, 2, 5, 7]


def attend_rows(decode_query_rows, key_cache, value_cache, new_keys, new_values, cache_len, step):
    row_count = decode_query_rows.shape[0]
    group_size = QH // KVH
    scaling = 1.0 / math.sqrt(HD)
    query_heads = decode_query_rows.reshape(row_count, KVH, group_size, HD)
    cached_keys = key_cache.reshape(row_count, CACHE, KVH, HD)
    cached_values = value_cache.reshape(row_count, CACHE, KVH, HD)
    fresh_keys = new_keys[: step + 1].reshape(step + 1, row_count, KVH, HD)
    fresh_values = new_values[: step + 1].reshape(step + 1, row_count, KVH, HD)
    previous_scores = (
        jnp.einsum("sjgd,stjd->sjgt", query_heads, cached_keys, preferred_element_type=jnp.float32)
        * scaling
    )
    new_scores = (
        jnp.einsum("sjgd,tsjd->sjgt", query_heads, fresh_keys, preferred_element_type=jnp.float32)
        * scaling
    )
    position = lax.broadcasted_iota(jnp.int32, (row_count, 1, 1, CACHE), 3)
    previous_scores = jnp.where(position < cache_len[:, None, None, None], previous_scores, -1e30)
    row_max = jnp.maximum(
        jnp.max(previous_scores, axis=-1, keepdims=True),
        jnp.max(new_scores, axis=-1, keepdims=True),
    )
    old_expo = jnp.exp(previous_scores - row_max)
    new_expo = jnp.exp(new_scores - row_max)
    denominator = jnp.sum(old_expo, axis=-1, keepdims=True) + jnp.sum(
        new_expo, axis=-1, keepdims=True
    )
    old_probs = (old_expo / denominator).astype(jnp.bfloat16)
    new_probs = (new_expo / denominator).astype(jnp.bfloat16)
    blended = jnp.einsum(
        "sjgt,stjd->sjgd", old_probs, cached_values, preferred_element_type=jnp.float32
    )
    blended = blended + jnp.einsum(
        "sjgt,tsjd->sjgd", new_probs, fresh_values, preferred_element_type=jnp.float32
    )
    return blended.reshape(row_count, QH * HD)


def norm_rows(hidden, norm_gain):
    mean_square = jnp.mean(hidden * hidden, axis=-1, keepdims=True)
    return (hidden * lax.rsqrt(mean_square + 1e-06) * norm_gain.astype(jnp.float32)).astype(
        jnp.bfloat16
    )


def exchange(array, axis, groups=None):
    return lax.all_to_all(
        array, axis, split_axis=0, concat_axis=0, tiled=True, axis_index_groups=groups
    )


def swap(array, turn):
    if turn == 0:
        return array
    return lax.ppermute(array, "exp", [(e, e ^ turn) for e in range(N_EXP)])


def routing_tables(chosen, scores, side, groups):
    gate_values = scores.astype(jnp.float32)
    gate_values = gate_values / jnp.sum(gate_values, axis=-1, keepdims=True)
    token = np.arange(TOK)
    source, step, seq = token // (STEPS * SEQ), token // SEQ % STEPS, token % SEQ
    order = source * SEQ + seq
    earlier = (step[:, None] == step[None, :]) & (order[None, :] < order[:, None])
    experts = 2 * lax.broadcasted_iota(jnp.int32, (1, 1, groups), 2) + side
    hits = (chosen[:, :, None] == experts).astype(jnp.float32)
    named = jnp.sum(hits, axis=1)
    weights = jnp.sum(hits * gate_values[:, :, None], axis=1)
    rank = jnp.dot(jnp.asarray(earlier, jnp.float32), named, preferred_element_type=jnp.float32)
    places = np.arange(STEPS * CAPE)
    rank = jnp.where(named > 0, rank, -1.0)
    wanted = np.where(
        step[:, None] == places[None, :] // CAPE, places[None, :] % CAPE, -2
    ).astype(np.float32)
    table = (rank[:, :, None] == wanted[:, None, :]).astype(jnp.float32)
    combine = (table * weights[:, :, None]).reshape(TOK, groups * STEPS * CAPE)
    return table.astype(jnp.bfloat16).reshape(TOK, groups * STEPS * CAPE), combine


def per_device(
    residual,
    queries,
    key_cache,
    value_cache,
    new_keys,
    new_values,
    cache_len,
    norm_gain,
    expert_ids,
    gate_scores,
    gate_weight,
    up_weight,
    down_weight,
):
    groups = lax.axis_size("rep")
    rows = groups * STEPS * CAPE
    me = lax.axis_index("exp")
    side = (me // 4 + me % 4) % 2

    routing = jnp.concatenate([expert_ids, gate_scores], axis=-1).reshape(1, STEPS * SEQ, 2 * TOPK)
    routing = exchange(jnp.broadcast_to(routing, (N_EXP, STEPS * SEQ, 2 * TOPK)), "exp")
    routing = routing.reshape(TOK, 2 * TOPK)

    units = [
        lax.dynamic_index_in_dim(gate_weight, side, 0, keepdims=False),
        lax.dynamic_index_in_dim(up_weight, side, 0, keepdims=False),
    ]
    borrowed = []
    for turn, near in enumerate(NEAR):
        third = jnp.concatenate(
            [
                lax.dynamic_slice(weight, (1 - side, turn * THIRD, 0), (1, THIRD, D))
                for weight in (gate_weight, up_weight)
            ]
        )
        borrowed.append(swap(third, near))
    down_blocks = []
    for turn in range(N_EXP):
        target = me ^ turn
        block = lax.dynamic_slice(
            down_weight, ((target // 4 + target % 4) % 2, 0, target // 2 * BLK), (1, UNITS, BLK)
        )[0]
        down_blocks.append(swap(block, turn))

    hidden, normed = [], []
    for step in range(STEPS):
        attention = attend_rows(
            queries[step], key_cache, value_cache, new_keys, new_values, cache_len, step
        )
        hidden.append(residual[step].astype(jnp.float32) + attention)
        normed.append(norm_rows(hidden[-1], norm_gain))
    normed = jnp.stack(normed).reshape(STEPS * SEQ, 4, 1, BLK)
    normed = jnp.broadcast_to(normed, (STEPS * SEQ, 4, 2, BLK)).reshape(STEPS * SEQ, N_EXP, BLK)
    normed, borrowed, routing = lax.optimization_barrier((normed, borrowed, routing))
    tokens = exchange(normed.transpose(1, 0, 2), "exp").reshape(TOK, BLK)

    table, combine = routing_tables(routing[:, :TOPK], routing[:, TOPK:], side, groups)

    def to_wire(array):
        return (
            array.reshape(groups, STEPS * CAPE, 2, BLK // 2)
            .transpose(0, 2, 1, 3)
            .reshape(groups, 2 * STEPS * CAPE, BLK // 2)
        )

    def from_wire(array):
        return (
            array.reshape(groups, 2, STEPS * CAPE, BLK // 2).transpose(0, 2, 1, 3).reshape(rows, BLK)
        )

    outbound = lax.dot_general(
        table, tokens, (((0,), (0,)), ((), ())), preferred_element_type=jnp.float32
    ).astype(jnp.bfloat16)
    inbound = from_wire(exchange(to_wire(outbound), "rep"))
    inbound, down_blocks = lax.optimization_barrier((inbound, down_blocks))
    slotted = exchange(
        jnp.broadcast_to(inbound[None], (4, rows, BLK)).reshape(4, rows, BLK), "exp", GROUPS
    )

    def project(which):
        weight = jnp.concatenate([units[which]] + [third[which] for third in borrowed], axis=0)
        total = jnp.zeros((rows, 2 * UNITS), jnp.float32)
        for q in range(4):
            total = total + lax.dot_general(
                slotted[q],
                weight[:, q * BLK : (q + 1) * BLK],
                (((1,), (1,)), ((), ())),
                preferred_element_type=jnp.float32,
            )
        return total

    activation = (jax.nn.silu(project(0)) * project(1)).astype(jnp.bfloat16)
    partial_value = jnp.zeros((rows, BLK), jnp.float32)
    for turn in SAME:
        down = jnp.concatenate(
            [down_blocks[turn]]
            + [
                down_blocks[turn ^ near][i * THIRD : (i + 1) * THIRD]
                for i, near in enumerate(NEAR)
            ],
            axis=0,
        )
        partial_value = partial_value + jnp.dot(
            swap(activation, turn), down, preferred_element_type=jnp.float32
        )
    partial_value = partial_value.astype(jnp.bfloat16)
    returned = from_wire(exchange(to_wire(partial_value), "rep"))
    weighted = jnp.dot(
        combine,
        returned.astype(jnp.float32),
        precision=lax.Precision.HIGHEST,
        preferred_element_type=jnp.float32,
    ).astype(jnp.bfloat16)
    expert_sum = exchange(weighted.reshape(N_EXP, STEPS * SEQ, BLK), "exp").astype(jnp.float32)
    expert_sum = expert_sum.reshape(4, 2, STEPS * SEQ, BLK).sum(axis=1)
    expert_sum = expert_sum.transpose(1, 0, 2).reshape(STEPS, SEQ, D)
    return (jnp.stack(hidden) + expert_sum).astype(jnp.bfloat16)


def solution(mesh):
    in_specs = (
        P(None, ("rep", "exp"), None),
        P(None, ("rep", "exp"), None),
        P(("rep", "exp"), None, None),
        P(("rep", "exp"), None, None),
        P(None, ("rep", "exp"), None),
        P(None, ("rep", "exp"), None),
        P(("rep", "exp")),
        P(),
        P(None, ("rep", "exp"), None),
        P(None, ("rep", "exp"), None),
        P("rep", "exp", None),
        P("rep", "exp", None),
        P("rep", "exp", None),
    )
    out_specs = P(None, ("rep", "exp"), None)
    return jax.shard_map(
        per_device, mesh=mesh, in_specs=in_specs, out_specs=out_specs, check_vma=False
    )
```

```python
import math

import numpy as np

import jax
import jax.numpy as jnp
from jax import lax
from jax.experimental import pallas as pl
from jax.experimental.pallas import tpu as pltpu
from jax.sharding import PartitionSpec as P

D = 4096
FF = 1536
HD = 128
QH = 32
KVH = 2
TOPK = 8
CAPE = 4
STEPS = 3
CACHE = 1024
N_EXP = 8
SEQ = 2
UNITS = FF // N_EXP
BLK = D // 4
HALF = BLK // 2
LOCAL = STEPS * SEQ
KEYS = N_EXP * 2 * LOCAL
PLACES = STEPS * CAPE
WIRE = 2 * PLACES


def attend_rows(decode_query_rows, key_cache, value_cache, new_keys, new_values, cache_len, step):
    row_count = decode_query_rows.shape[0]
    group_size = QH // KVH
    scaling = 1.0 / math.sqrt(HD)
    query_heads = decode_query_rows.reshape(row_count, KVH, group_size, HD)
    cached_keys = key_cache.reshape(row_count, CACHE, KVH, HD)
    cached_values = value_cache.reshape(row_count, CACHE, KVH, HD)
    fresh_keys = new_keys[: step + 1].reshape(step + 1, row_count, KVH, HD)
    fresh_values = new_values[: step + 1].reshape(step + 1, row_count, KVH, HD)
    previous_scores = (
        jnp.einsum("sjgd,stjd->sjgt", query_heads, cached_keys, preferred_element_type=jnp.float32)
        * scaling
    )
    new_scores = (
        jnp.einsum("sjgd,tsjd->sjgt", query_heads, fresh_keys, preferred_element_type=jnp.float32)
        * scaling
    )
    position = lax.broadcasted_iota(jnp.int32, (row_count, 1, 1, CACHE), 3)
    previous_scores = jnp.where(position < cache_len[:, None, None, None], previous_scores, -1e30)
    row_max = jnp.maximum(
        jnp.max(previous_scores, axis=-1, keepdims=True),
        jnp.max(new_scores, axis=-1, keepdims=True),
    )
    old_expo = jnp.exp(previous_scores - row_max)
    new_expo = jnp.exp(new_scores - row_max)
    denominator = jnp.sum(old_expo, axis=-1, keepdims=True) + jnp.sum(
        new_expo, axis=-1, keepdims=True
    )
    old_probs = (old_expo / denominator).astype(jnp.bfloat16)
    new_probs = (new_expo / denominator).astype(jnp.bfloat16)
    blended = jnp.einsum(
        "sjgt,stjd->sjgd", old_probs, cached_values, preferred_element_type=jnp.float32
    )
    blended = blended + jnp.einsum(
        "sjgt,tsjd->sjgd", new_probs, fresh_values, preferred_element_type=jnp.float32
    )
    return blended.reshape(row_count, QH * HD)


def norm_rows(hidden, norm_gain):
    mean_square = jnp.mean(hidden * hidden, axis=-1, keepdims=True)
    return (hidden * lax.rsqrt(mean_square + 1e-06) * norm_gain.astype(jnp.float32)).astype(
        jnp.bfloat16
    )


def exchange(array, axis):
    return lax.all_to_all(array, axis, split_axis=0, concat_axis=0, tiled=True)


def shift(array, step):
    pairs = [(e, e // 4 * 4 + (e + step) % 4) for e in range(N_EXP)]
    return lax.ppermute(array, "exp", pairs)


def across(array):
    return lax.ppermute(array, "exp", [(e, e ^ 4) for e in range(N_EXP)])


def ring(block):
    half = block.shape[0] // 2
    below, above = shift(block, 1), shift(block, -1)
    return block, below, above, shift(below[:half], 1), shift(above[half:], -1)


def routing_tables(chosen, scores, side, groups):
    gate_values = scores.astype(jnp.float32)
    gate_values = gate_values / jnp.sum(gate_values, axis=-1, keepdims=True)
    key = np.arange(KEYS)
    source, half, step, seq = (
        key // (2 * LOCAL),
        key // LOCAL % 2,
        key % LOCAL // SEQ,
        key % SEQ,
    )
    order = source * SEQ + seq
    earlier = (
        (step[:, None] == step[None, :])
        & (half[:, None] == half[None, :])
        & (order[None, :] < order[:, None])
    )
    experts = 2 * lax.broadcasted_iota(jnp.int32, (1, 1, groups), 2) + side
    hits = (chosen[:, :, None] == experts).astype(jnp.float32)
    named = jnp.sum(hits, axis=1)
    weights = jnp.sum(hits * gate_values[:, :, None], axis=1)
    rank = jnp.dot(jnp.asarray(earlier, jnp.float32), named, preferred_element_type=jnp.float32)
    rank = jnp.where(named > 0, rank, -1.0)
    place = np.arange(WIRE)
    wanted = np.where(
        (half[:, None] == place[None, :] // PLACES)
        & (step[:, None] == place[None, :] % PLACES // CAPE),
        place[None, :] % CAPE,
        -2,
    ).astype(np.float32)
    table = (rank[:, :, None] == wanted[:, None, :]).astype(jnp.float32)
    combine = (table * weights[:, :, None]).reshape(KEYS, groups * WIRE)
    return table.astype(jnp.bfloat16).reshape(KEYS, groups * WIRE), combine


def contract_last(left, right):
    return lax.dot_general(
        left, right, (((1,), (1,)), ((), ())), preferred_element_type=jnp.float32
    )


def expand_kernel(
    where,
    own_rows,
    below_rows,
    above_rows,
    far_low,
    far_high,
    own_gate,
    own_up,
    lent_gate,
    lent_up,
    out,
    gate_total,
    up_total,
):
    turn = pl.program_id(0)
    gate_block = jnp.concatenate([own_gate[0], lent_gate[...]], axis=0)
    up_block = jnp.concatenate([own_up[0], lent_up[...]], axis=0)

    @pl.when(turn == 0)
    def _():
        gate_total[...] = contract_last(own_rows[...], gate_block)
        up_total[...] = contract_last(own_rows[...], up_block)

    @pl.when(turn == 1)
    def _():
        gate_total[...] += contract_last(below_rows[...], gate_block)
        up_total[...] += contract_last(below_rows[...], up_block)

    @pl.when(turn == 2)
    def _():
        gate_total[...] += contract_last(above_rows[...], gate_block)
        up_total[...] += contract_last(above_rows[...], up_block)

    @pl.when(turn == 3)
    def _():
        half = far_low.shape[0]
        for start, rows in ((0, far_low), (half, far_high)):
            span = pl.ds(start, half)
            gate = gate_total[span, :] + contract_last(rows[...], gate_block)
            up = up_total[span, :] + contract_last(rows[...], up_block)
            out[span, :] = (gate / (1.0 + jnp.exp(-gate)) * up).astype(jnp.bfloat16)


def expand(where, rows, gate_weight, up_weight, lent_gate, lent_up):
    count = rows[0].shape[0]

    def column(turn, where):
        return (where[1] + jnp.where(turn == 1, 3, jnp.where(turn == 2, 1, turn - turn // 3))) % 4

    def whole(shape):
        return pl.BlockSpec(shape, lambda turn, where: (0, 0))

    own = pl.BlockSpec((1, UNITS, BLK), lambda turn, where: (where[0], 0, column(turn, where)))
    lent = pl.BlockSpec((UNITS, BLK), lambda turn, where: (0, column(turn, where)))
    return pl.pallas_call(
        expand_kernel,
        out_shape=jax.ShapeDtypeStruct((count, 2 * UNITS), jnp.bfloat16),
        grid_spec=pltpu.PrefetchScalarGridSpec(
            num_scalar_prefetch=1,
            grid=(4,),
            in_specs=[whole(array.shape) for array in rows] + [own, own, lent, lent],
            out_specs=whole((count, 2 * UNITS)),
            scratch_shapes=[
                pltpu.VMEM((count, 2 * UNITS), jnp.float32),
                pltpu.VMEM((count, 2 * UNITS), jnp.float32),
            ],
        ),
        compiler_params=pltpu.CompilerParams(
            dimension_semantics=("arbitrary",), vmem_limit_bytes=32 << 20
        ),
        cost_estimate=pl.CostEstimate(
            flops=8 * count * UNITS * D,
            bytes_accessed=2 * count * D + 8 * UNITS * D + 4 * count * UNITS,
            transcendentals=2 * count * UNITS,
        ),
        name="expand",
    )(where, *rows, gate_weight, up_weight, lent_gate, lent_up)


def contract_kernel(own, below, above, far_low, far_high, w_own, w_below, w_above, w_far, out):
    half = far_low.shape[0]
    for start, far in ((0, far_low), (half, far_high)):
        span = pl.ds(start, half)
        total = jnp.dot(own[span, :], w_own[...], preferred_element_type=jnp.float32)
        total += jnp.dot(below[span, :], w_below[...], preferred_element_type=jnp.float32)
        total += jnp.dot(above[span, :], w_above[...], preferred_element_type=jnp.float32)
        total += jnp.dot(far[...], w_far[...], preferred_element_type=jnp.float32)
        out[span, :] = total.astype(jnp.bfloat16)


def contract(acts, weights):
    count = acts[0].shape[0]
    return pl.pallas_call(
        contract_kernel,
        out_shape=jax.ShapeDtypeStruct((count, BLK), jnp.bfloat16),
        compiler_params=pltpu.CompilerParams(vmem_limit_bytes=32 << 20),
        cost_estimate=pl.CostEstimate(
            flops=2 * count * FF * BLK,
            bytes_accessed=2 * (count * FF + FF * BLK + count * BLK),
            transcendentals=0,
        ),
        name="contract",
    )(*acts, *weights)


def per_device(
    residual,
    queries,
    key_cache,
    value_cache,
    new_keys,
    new_values,
    cache_len,
    norm_gain,
    expert_ids,
    gate_scores,
    gate_weight,
    up_weight,
    down_weight,
):
    groups = lax.axis_size("rep")
    rows = groups * PLACES
    me = lax.axis_index("exp")
    side, place = me // 4, me % 4

    routing = jnp.concatenate([expert_ids, gate_scores], axis=-1).reshape(1, LOCAL, 2 * TOPK)
    routing = exchange(jnp.broadcast_to(routing, (N_EXP, LOCAL, 2 * TOPK)), "exp")
    routing = jnp.broadcast_to(routing[:, None], (N_EXP, 2, LOCAL, 2 * TOPK))
    routing = routing.reshape(KEYS, 2 * TOPK)

    lent_down, lent_gate, lent_up = [
        across(lax.dynamic_index_in_dim(weight, 1 - side, 0, keepdims=False))
        for weight in (down_weight, gate_weight, up_weight)
    ]

    hidden, normed = [], []
    for step in range(STEPS):
        attention = attend_rows(
            queries[step], key_cache, value_cache, new_keys, new_values, cache_len, step
        )
        hidden.append(residual[step].astype(jnp.float32) + attention)
        normed.append(norm_rows(hidden[-1], norm_gain))
    normed = jnp.stack(normed).reshape(LOCAL, 4, 2, HALF).transpose(1, 2, 0, 3)
    normed = jnp.broadcast_to(
        normed.reshape(1, 4, 2 * LOCAL, HALF), (2, 4, 2 * LOCAL, HALF)
    ).reshape(N_EXP, 2 * LOCAL, HALF)
    tokens = exchange(normed, "exp").reshape(KEYS, HALF)
    table, combine = routing_tables(routing[:, :TOPK], routing[:, TOPK:], side, groups)
    outbound = lax.dot_general(
        table, tokens, (((0,), (0,)), ((), ())), preferred_element_type=jnp.float32
    ).astype(jnp.bfloat16)

    outbound, lent_down = lax.optimization_barrier((outbound, lent_down))

    def quarter(step):
        start = (place + step) % 4 * BLK
        kept = lax.dynamic_slice(down_weight, (side, 0, start), (1, UNITS, BLK))[0]
        return jnp.concatenate([kept, lax.dynamic_slice(lent_down, (0, start), (UNITS, BLK))])

    down = [quarter(0)] + [shift(quarter(step), step) for step in (1, -1, 2)]

    inbound = exchange(outbound.reshape(groups, WIRE, HALF), "rep")
    inbound, down, lent_gate = lax.optimization_barrier((inbound, down, lent_gate))
    slotted = inbound.reshape(groups, 2, PLACES, HALF).transpose(0, 2, 1, 3).reshape(rows, BLK)
    where = jnp.stack([side, place])
    activation = expand(where, ring(slotted), gate_weight, up_weight, lent_gate, lent_up)
    partial_value = contract(ring(activation), down)
    partial_value = partial_value.reshape(groups, PLACES, 2, HALF).transpose(0, 2, 1, 3)
    returned = exchange(partial_value.reshape(groups, WIRE, HALF), "rep")
    weighted = jnp.dot(
        combine,
        returned.reshape(groups * WIRE, HALF).astype(jnp.float32),
        precision=lax.Precision.HIGHEST,
        preferred_element_type=jnp.float32,
    ).astype(jnp.bfloat16)
    expert_sum = exchange(weighted.reshape(N_EXP, 2 * LOCAL, HALF), "exp").astype(jnp.float32)
    expert_sum = expert_sum.reshape(2, 4, 2, LOCAL, HALF).sum(axis=0)
    expert_sum = expert_sum.transpose(2, 0, 1, 3).reshape(STEPS, SEQ, D)
    return (jnp.stack(hidden) + expert_sum).astype(jnp.bfloat16)


def solution(mesh):
    in_specs = (
        P(None, ("rep", "exp"), None),
        P(None, ("rep", "exp"), None),
        P(("rep", "exp"), None, None),
        P(("rep", "exp"), None, None),
        P(None, ("rep", "exp"), None),
        P(None, ("rep", "exp"), None),
        P(("rep", "exp")),
        P(),
        P(None, ("rep", "exp"), None),
        P(None, ("rep", "exp"), None),
        P("rep", "exp", None),
        P("rep", "exp", None),
        P("rep", "exp", None),
    )
    out_specs = P(None, ("rep", "exp"), None)
    return jax.shard_map(
        per_device, mesh=mesh, in_specs=in_specs, out_specs=out_specs, check_vma=False
    )
```

```python
import math

import numpy as np

import jax
import jax.numpy as jnp
from jax import lax
from jax.experimental import pallas as pl
from jax.experimental.pallas import tpu as pltpu
from jax.sharding import PartitionSpec as P

D = 4096
FF = 1536
HD = 128
QH = 32
KVH = 2
TOPK = 8
CAPE = 4
STEPS = 3
CACHE = 1024
N_EXP = 8
SEQ = 2
UNITS = FF // N_EXP
BLK = D // 4
HALF = BLK // 2
LOCAL = STEPS * SEQ
KEYS = N_EXP * 2 * LOCAL
PLACES = STEPS * CAPE
WIRE = 2 * PLACES


def attend_rows(decode_query_rows, key_cache, value_cache, new_keys, new_values, cache_len, step):
    row_count = decode_query_rows.shape[0]
    group_size = QH // KVH
    scaling = 1.0 / math.sqrt(HD)
    query_heads = decode_query_rows.reshape(row_count, KVH, group_size, HD)
    cached_keys = key_cache.reshape(row_count, CACHE, KVH, HD)
    cached_values = value_cache.reshape(row_count, CACHE, KVH, HD)
    fresh_keys = new_keys[: step + 1].reshape(step + 1, row_count, KVH, HD)
    fresh_values = new_values[: step + 1].reshape(step + 1, row_count, KVH, HD)
    previous_scores = (
        jnp.einsum("sjgd,stjd->sjgt", query_heads, cached_keys, preferred_element_type=jnp.float32)
        * scaling
    )
    new_scores = (
        jnp.einsum("sjgd,tsjd->sjgt", query_heads, fresh_keys, preferred_element_type=jnp.float32)
        * scaling
    )
    position = lax.broadcasted_iota(jnp.int32, (row_count, 1, 1, CACHE), 3)
    previous_scores = jnp.where(position < cache_len[:, None, None, None], previous_scores, -1e30)
    row_max = jnp.maximum(
        jnp.max(previous_scores, axis=-1, keepdims=True),
        jnp.max(new_scores, axis=-1, keepdims=True),
    )
    old_expo = jnp.exp(previous_scores - row_max)
    new_expo = jnp.exp(new_scores - row_max)
    denominator = jnp.sum(old_expo, axis=-1, keepdims=True) + jnp.sum(
        new_expo, axis=-1, keepdims=True
    )
    old_probs = (old_expo / denominator).astype(jnp.bfloat16)
    new_probs = (new_expo / denominator).astype(jnp.bfloat16)
    blended = jnp.einsum(
        "sjgt,stjd->sjgd", old_probs, cached_values, preferred_element_type=jnp.float32
    )
    blended = blended + jnp.einsum(
        "sjgt,tsjd->sjgd", new_probs, fresh_values, preferred_element_type=jnp.float32
    )
    return blended.reshape(row_count, QH * HD)


def norm_rows(hidden, norm_gain):
    mean_square = jnp.mean(hidden * hidden, axis=-1, keepdims=True)
    return (hidden * lax.rsqrt(mean_square + 1e-06) * norm_gain.astype(jnp.float32)).astype(
        jnp.bfloat16
    )


def exchange(array, axis):
    return lax.all_to_all(array, axis, split_axis=0, concat_axis=0, tiled=True)


def shift(array, step):
    pairs = [(e, e // 4 * 4 + (e + step) % 4) for e in range(N_EXP)]
    return lax.ppermute(array, "exp", pairs)


def across(array):
    return lax.ppermute(array, "exp", [(e, e ^ 4) for e in range(N_EXP)])


def ring(block):
    half = block.shape[0] // 2
    below, above = shift(block, 1), shift(block, -1)
    return block, below, above, shift(below[:half], 1), shift(above[half:], -1)


def routing_tables(chosen, scores, side, groups):
    gate_values = scores.astype(jnp.float32)
    gate_values = gate_values / jnp.sum(gate_values, axis=-1, keepdims=True)
    key = np.arange(KEYS)
    source, half, step, seq = (
        key // (2 * LOCAL),
        key // LOCAL % 2,
        key % LOCAL // SEQ,
        key % SEQ,
    )
    order = source * SEQ + seq
    earlier = (
        (step[:, None] == step[None, :])
        & (half[:, None] == half[None, :])
        & (order[None, :] < order[:, None])
    )
    experts = 2 * lax.broadcasted_iota(jnp.int32, (1, 1, groups), 2) + side
    hits = (chosen[:, :, None] == experts).astype(jnp.float32)
    named = jnp.sum(hits, axis=1)
    weights = jnp.sum(hits * gate_values[:, :, None], axis=1)
    rank = jnp.dot(jnp.asarray(earlier, jnp.float32), named, preferred_element_type=jnp.float32)
    rank = jnp.where(named > 0, rank, -1.0)
    place = np.arange(WIRE)
    wanted = np.where(
        (half[:, None] == place[None, :] // PLACES)
        & (step[:, None] == place[None, :] % PLACES // CAPE),
        place[None, :] % CAPE,
        -2,
    ).astype(np.float32)
    table = (rank[:, :, None] == wanted[:, None, :]).astype(jnp.float32)
    combine = (table * weights[:, :, None]).reshape(KEYS, groups * WIRE)
    return table.astype(jnp.bfloat16).reshape(KEYS, groups * WIRE), combine


def contract_last(left, right):
    return lax.dot_general(
        left, right, (((1,), (1,)), ((), ())), preferred_element_type=jnp.float32
    )


def expand_near_kernel(
    where,
    own_rows,
    below_rows,
    above_rows,
    own_gate,
    own_up,
    lent_gate_low,
    lent_gate_high,
    lent_up,
    gate_total,
    up_total,
):
    turn = pl.program_id(0)
    gate_block = jnp.concatenate([own_gate[0], lent_gate_low[...], lent_gate_high[...]], axis=0)
    up_block = jnp.concatenate([own_up[0], lent_up[...]], axis=0)

    @pl.when(turn == 0)
    def _():
        gate_total[...] = contract_last(own_rows[...], gate_block)
        up_total[...] = contract_last(own_rows[...], up_block)

    @pl.when(turn == 1)
    def _():
        gate_total[...] += contract_last(below_rows[...], gate_block)
        up_total[...] += contract_last(below_rows[...], up_block)

    @pl.when(turn == 2)
    def _():
        gate_total[...] += contract_last(above_rows[...], gate_block)
        up_total[...] += contract_last(above_rows[...], up_block)


def expand_far_kernel(
    where,
    far_low,
    far_high,
    gate_total,
    up_total,
    own_gate,
    own_up,
    lent_gate_low,
    lent_gate_high,
    lent_up,
    out,
):
    gate_block = jnp.concatenate([own_gate[0], lent_gate_low[...], lent_gate_high[...]], axis=0)
    up_block = jnp.concatenate([own_up[0], lent_up[...]], axis=0)
    half = far_low.shape[0]
    for start, rows in ((0, far_low), (half, far_high)):
        span = pl.ds(start, half)
        gate = gate_total[span, :] + contract_last(rows[...], gate_block)
        up = up_total[span, :] + contract_last(rows[...], up_block)
        out[span, :] = (gate / (1.0 + jnp.exp(-gate)) * up).astype(jnp.bfloat16)


def expand(where, rows, weights):
    count = rows[0].shape[0]

    def near_column(turn, where):
        return (where[1] + jnp.where(turn == 1, 3, jnp.where(turn == 2, 1, 0))) % 4

    def far_column(turn, where):
        return (where[1] + 2) % 4

    def whole(shape):
        return pl.BlockSpec(shape, lambda turn, where: (0, 0))

    def call(kernel, name, steps, column, inputs, out_shape):
        own = pl.BlockSpec((1, UNITS, BLK), lambda turn, where: (where[0], 0, column(turn, where)))
        lent = pl.BlockSpec((UNITS, BLK), lambda turn, where: (0, column(turn, where)))
        part = pl.BlockSpec((UNITS // 2, BLK), lambda turn, where: (0, column(turn, where)))
        outs = jax.tree.leaves(out_shape)
        out_specs = jax.tree.unflatten(
            jax.tree.structure(out_shape), [whole(leaf.shape) for leaf in outs]
        )
        return pl.pallas_call(
            kernel,
            out_shape=out_shape,
            grid_spec=pltpu.PrefetchScalarGridSpec(
                num_scalar_prefetch=1,
                grid=(steps,),
                in_specs=[whole(array.shape) for array in inputs] + [own, own, part, part, lent],
                out_specs=out_specs,
            ),
            compiler_params=pltpu.CompilerParams(
                dimension_semantics=("arbitrary",), vmem_limit_bytes=32 << 20
            ),
            cost_estimate=pl.CostEstimate(
                flops=8 * count * UNITS * BLK * steps,
                bytes_accessed=steps * BLK * (2 * count + 8 * UNITS) + 16 * count * UNITS,
                transcendentals=0,
            ),
            name=name,
        )(where, *inputs, *weights)

    total = jax.ShapeDtypeStruct((count, 2 * UNITS), jnp.float32)
    totals = call(expand_near_kernel, "expand_near", 3, near_column, rows[:3], (total, total))
    out = jax.ShapeDtypeStruct((count, 2 * UNITS), jnp.bfloat16)
    return call(
        expand_far_kernel, "expand_far", 1, far_column, (*rows[3:], *totals), out
    )


def contract_kernel(own, below, above, far_low, far_high, w_own, w_below, w_above, w_far, lent, out):
    half = far_low.shape[0]
    blocks = [
        jnp.concatenate([kept[0], lent[turn * UNITS : (turn + 1) * UNITS]], axis=0)
        for turn, kept in enumerate((w_own, w_below, w_above, w_far))
    ]
    for start, far in ((0, far_low), (half, far_high)):
        span = pl.ds(start, half)
        total = jnp.dot(own[span, :], blocks[0], preferred_element_type=jnp.float32)
        total += jnp.dot(below[span, :], blocks[1], preferred_element_type=jnp.float32)
        total += jnp.dot(above[span, :], blocks[2], preferred_element_type=jnp.float32)
        total += jnp.dot(far[...], blocks[3], preferred_element_type=jnp.float32)
        out[span, :] = total.astype(jnp.bfloat16)


def contract(acts, kept, lent):
    count = acts[0].shape[0]
    return pl.pallas_call(
        contract_kernel,
        out_shape=jax.ShapeDtypeStruct((count, BLK), jnp.bfloat16),
        compiler_params=pltpu.CompilerParams(vmem_limit_bytes=32 << 20),
        cost_estimate=pl.CostEstimate(
            flops=2 * count * FF * BLK,
            bytes_accessed=2 * (count * FF + FF * BLK + count * BLK),
            transcendentals=0,
        ),
        name="contract",
    )(*acts, *kept, lent)


def per_device(
    residual,
    queries,
    key_cache,
    value_cache,
    new_keys,
    new_values,
    cache_len,
    norm_gain,
    expert_ids,
    gate_scores,
    gate_weight,
    up_weight,
    down_weight,
):
    groups = lax.axis_size("rep")
    rows = groups * PLACES
    me = lax.axis_index("exp")
    side, place = me // 4, me % 4

    routing = jnp.concatenate([expert_ids, gate_scores], axis=-1).reshape(1, LOCAL, 2 * TOPK)
    routing = exchange(jnp.broadcast_to(routing, (N_EXP, LOCAL, 2 * TOPK)), "exp")
    routing = jnp.broadcast_to(routing[:, None], (N_EXP, 2, LOCAL, 2 * TOPK))
    routing = routing.reshape(KEYS, 2 * TOPK)

    half = UNITS // 2
    lent_gate_low = across(lax.dynamic_slice(gate_weight, (1 - side, 0, 0), (1, half, D))[0])

    hidden, normed = [], []
    for step in range(STEPS):
        attention = attend_rows(
            queries[step], key_cache, value_cache, new_keys, new_values, cache_len, step
        )
        hidden.append(residual[step].astype(jnp.float32) + attention)
        normed.append(norm_rows(hidden[-1], norm_gain))
    normed = jnp.stack(normed).reshape(LOCAL, 4, 2, HALF).transpose(1, 2, 0, 3)
    normed = jnp.broadcast_to(
        normed.reshape(1, 4, 2 * LOCAL, HALF), (2, 4, 2 * LOCAL, HALF)
    ).reshape(N_EXP, 2 * LOCAL, HALF)
    normed, lent_gate_low = lax.optimization_barrier((normed, lent_gate_low))
    tokens = exchange(normed, "exp").reshape(KEYS, HALF)
    table, combine = routing_tables(routing[:, :TOPK], routing[:, TOPK:], side, groups)
    outbound = lax.dot_general(
        table, tokens, (((0,), (0,)), ((), ())), preferred_element_type=jnp.float32
    ).astype(jnp.bfloat16)

    outbound, gate_late, up_late, down_late = lax.optimization_barrier(
        (outbound, gate_weight, up_weight, down_weight)
    )
    inbound = exchange(outbound.reshape(groups, WIRE, HALF), "rep")

    def quarter(step):
        start = (place + step) % 4 * BLK
        return jnp.concatenate(
            [
                lax.dynamic_slice(down_late, (expert, 0, start), (1, UNITS, BLK))
                for expert in (side, 1 - side)
            ]
        )

    kept = [quarter(0)] + [shift(quarter(step), step) for step in (1, -1, 2)]
    lent_gate_high = across(lax.dynamic_slice(gate_late, (1 - side, half, 0), (1, half, D))[0])
    lent_up = across(lax.dynamic_index_in_dim(up_late, 1 - side, 0, keepdims=False))
    inbound, kept, lent_gate_high = lax.optimization_barrier((inbound, kept, lent_gate_high))
    lent_down = across(jnp.concatenate([block[1] for block in kept]))
    slotted = inbound.reshape(groups, 2, PLACES, HALF).transpose(0, 2, 1, 3).reshape(rows, BLK)
    where = jnp.stack([side, place])
    weights = (gate_weight, up_weight, lent_gate_low, lent_gate_high, lent_up)
    activation = expand(where, ring(slotted), weights)
    partial_value = contract(ring(activation), kept, lent_down)
    partial_value = partial_value.reshape(groups, PLACES, 2, HALF).transpose(0, 2, 1, 3)
    returned = exchange(partial_value.reshape(groups, WIRE, HALF), "rep")
    weighted = jnp.dot(
        combine,
        returned.reshape(groups * WIRE, HALF).astype(jnp.float32),
        precision=lax.Precision.HIGHEST,
        preferred_element_type=jnp.float32,
    ).astype(jnp.bfloat16)
    expert_sum = exchange(weighted.reshape(N_EXP, 2 * LOCAL, HALF), "exp").astype(jnp.float32)
    expert_sum = expert_sum.reshape(2, 4, 2, LOCAL, HALF).sum(axis=0)
    expert_sum = expert_sum.transpose(2, 0, 1, 3).reshape(STEPS, SEQ, D)
    return (jnp.stack(hidden) + expert_sum).astype(jnp.bfloat16)


def solution(mesh):
    in_specs = (
        P(None, ("rep", "exp"), None),
        P(None, ("rep", "exp"), None),
        P(("rep", "exp"), None, None),
        P(("rep", "exp"), None, None),
        P(None, ("rep", "exp"), None),
        P(None, ("rep", "exp"), None),
        P(("rep", "exp")),
        P(),
        P(None, ("rep", "exp"), None),
        P(None, ("rep", "exp"), None),
        P("rep", "exp", None),
        P("rep", "exp", None),
        P("rep", "exp", None),
    )
    out_specs = P(None, ("rep", "exp"), None)
    return jax.shard_map(
        per_device, mesh=mesh, in_specs=in_specs, out_specs=out_specs, check_vma=False
    )
```

```python
import math

import numpy as np

import jax
import jax.numpy as jnp
from jax import lax
from jax.experimental import pallas as pl
from jax.experimental.pallas import tpu as pltpu
from jax.sharding import PartitionSpec as P

D = 4096
FF = 1536
HD = 128
QH = 32
KVH = 2
TOPK = 8
CAPE = 4
STEPS = 3
CACHE = 1024
N_EXP = 8
SEQ = 2
UNITS = FF // N_EXP
BLK = D // 4
HALF = BLK // 2
LOCAL = STEPS * SEQ
KEYS = N_EXP * 2 * LOCAL
PLACES = STEPS * CAPE
WIRE = 2 * PLACES


def attend_rows(decode_query_rows, key_cache, value_cache, new_keys, new_values, cache_len, step):
    row_count = decode_query_rows.shape[0]
    group_size = QH // KVH
    scaling = 1.0 / math.sqrt(HD)
    query_heads = decode_query_rows.reshape(row_count, KVH, group_size, HD)
    cached_keys = key_cache.reshape(row_count, CACHE, KVH, HD)
    cached_values = value_cache.reshape(row_count, CACHE, KVH, HD)
    fresh_keys = new_keys[: step + 1].reshape(step + 1, row_count, KVH, HD)
    fresh_values = new_values[: step + 1].reshape(step + 1, row_count, KVH, HD)
    previous_scores = (
        jnp.einsum("sjgd,stjd->sjgt", query_heads, cached_keys, preferred_element_type=jnp.float32)
        * scaling
    )
    new_scores = (
        jnp.einsum("sjgd,tsjd->sjgt", query_heads, fresh_keys, preferred_element_type=jnp.float32)
        * scaling
    )
    position = lax.broadcasted_iota(jnp.int32, (row_count, 1, 1, CACHE), 3)
    previous_scores = jnp.where(position < cache_len[:, None, None, None], previous_scores, -1e30)
    row_max = jnp.maximum(
        jnp.max(previous_scores, axis=-1, keepdims=True),
        jnp.max(new_scores, axis=-1, keepdims=True),
    )
    old_expo = jnp.exp(previous_scores - row_max)
    new_expo = jnp.exp(new_scores - row_max)
    denominator = jnp.sum(old_expo, axis=-1, keepdims=True) + jnp.sum(
        new_expo, axis=-1, keepdims=True
    )
    old_probs = (old_expo / denominator).astype(jnp.bfloat16)
    new_probs = (new_expo / denominator).astype(jnp.bfloat16)
    blended = jnp.einsum(
        "sjgt,stjd->sjgd", old_probs, cached_values, preferred_element_type=jnp.float32
    )
    blended = blended + jnp.einsum(
        "sjgt,tsjd->sjgd", new_probs, fresh_values, preferred_element_type=jnp.float32
    )
    return blended.reshape(row_count, QH * HD)


def norm_rows(hidden, norm_gain):
    mean_square = jnp.mean(hidden * hidden, axis=-1, keepdims=True)
    return (hidden * lax.rsqrt(mean_square + 1e-06) * norm_gain.astype(jnp.float32)).astype(
        jnp.bfloat16
    )


def exchange(array, axis):
    return lax.all_to_all(array, axis, split_axis=0, concat_axis=0, tiled=True)


def shift(array, step):
    pairs = [(e, e // 4 * 4 + (e + step) % 4) for e in range(N_EXP)]
    return lax.ppermute(array, "exp", pairs)


def across(array):
    return lax.ppermute(array, "exp", [(e, e ^ 4) for e in range(N_EXP)])


def ring(block):
    half = block.shape[0] // 2
    below, above = shift(block, 1), shift(block, -1)
    return block, below, above, shift(below[:half], 1), shift(above[half:], -1)


def routing_tables(chosen, scores, side, groups):
    gate_values = scores.astype(jnp.float32)
    gate_values = gate_values / jnp.sum(gate_values, axis=-1, keepdims=True)
    key = np.arange(KEYS)
    source, half, step, seq = (
        key // (2 * LOCAL),
        key // LOCAL % 2,
        key % LOCAL // SEQ,
        key % SEQ,
    )
    order = source * SEQ + seq
    earlier = (
        (step[:, None] == step[None, :])
        & (half[:, None] == half[None, :])
        & (order[None, :] < order[:, None])
    )
    experts = 2 * lax.broadcasted_iota(jnp.int32, (1, 1, groups), 2) + side
    hits = (chosen[:, :, None] == experts).astype(jnp.float32)
    named = jnp.sum(hits, axis=1)
    weights = jnp.sum(hits * gate_values[:, :, None], axis=1)
    rank = jnp.dot(jnp.asarray(earlier, jnp.float32), named, preferred_element_type=jnp.float32)
    rank = jnp.where(named > 0, rank, -1.0)
    place = np.arange(WIRE)
    wanted = np.where(
        (half[:, None] == place[None, :] // PLACES)
        & (step[:, None] == place[None, :] % PLACES // CAPE),
        place[None, :] % CAPE,
        -2,
    ).astype(np.float32)
    table = (rank[:, :, None] == wanted[:, None, :]).astype(jnp.float32)
    combine = (table * weights[:, :, None]).reshape(KEYS, groups * WIRE)
    return table.astype(jnp.bfloat16).reshape(KEYS, groups * WIRE), combine


def contract_last(left, right):
    return lax.dot_general(
        left, right, (((1,), (1,)), ((), ())), preferred_element_type=jnp.float32
    )


def expand_near_kernel(
    where,
    own_rows,
    below_rows,
    above_rows,
    own_gate,
    own_up,
    lent_gate_low,
    lent_gate_high,
    lent_up,
    gate_total,
    up_total,
):
    turn = pl.program_id(0)
    gate_block = jnp.concatenate([own_gate[0], lent_gate_low[...], lent_gate_high[...]], axis=0)
    up_block = jnp.concatenate([own_up[0], lent_up[...]], axis=0)

    @pl.when(turn == 0)
    def _():
        gate_total[...] = contract_last(own_rows[...], gate_block)
        up_total[...] = contract_last(own_rows[...], up_block)

    @pl.when(turn == 1)
    def _():
        gate_total[...] += contract_last(below_rows[...], gate_block)
        up_total[...] += contract_last(below_rows[...], up_block)

    @pl.when(turn == 2)
    def _():
        gate_total[...] += contract_last(above_rows[...], gate_block)
        up_total[...] += contract_last(above_rows[...], up_block)


def expand_far_kernel(
    where,
    far_low,
    far_high,
    gate_total,
    up_total,
    own_gate,
    own_up,
    lent_gate_low,
    lent_gate_high,
    lent_up,
    out,
):
    gate_block = jnp.concatenate([own_gate[0], lent_gate_low[...], lent_gate_high[...]], axis=0)
    up_block = jnp.concatenate([own_up[0], lent_up[...]], axis=0)
    half = far_low.shape[0]
    for start, rows in ((0, far_low), (half, far_high)):
        span = pl.ds(start, half)
        gate = gate_total[span, :] + contract_last(rows[...], gate_block)
        up = up_total[span, :] + contract_last(rows[...], up_block)
        out[span, :] = (gate / (1.0 + jnp.exp(-gate)) * up).astype(jnp.bfloat16)


def expand(where, rows, weights):
    count = rows[0].shape[0]

    def near_column(turn, where):
        return (where[1] + jnp.where(turn == 1, 3, jnp.where(turn == 2, 1, 0))) % 4

    def far_column(turn, where):
        return (where[1] + 2) % 4

    def whole(shape):
        return pl.BlockSpec(shape, lambda turn, where: (0, 0))

    def call(kernel, name, steps, column, inputs, out_shape):
        own = pl.BlockSpec((1, UNITS, BLK), lambda turn, where: (where[0], 0, column(turn, where)))
        lent = pl.BlockSpec((UNITS, BLK), lambda turn, where: (0, column(turn, where)))
        part = pl.BlockSpec((UNITS // 2, BLK), lambda turn, where: (0, column(turn, where)))
        outs = jax.tree.leaves(out_shape)
        out_specs = jax.tree.unflatten(
            jax.tree.structure(out_shape), [whole(leaf.shape) for leaf in outs]
        )
        return pl.pallas_call(
            kernel,
            out_shape=out_shape,
            grid_spec=pltpu.PrefetchScalarGridSpec(
                num_scalar_prefetch=1,
                grid=(steps,),
                in_specs=[whole(array.shape) for array in inputs] + [own, own, part, part, lent],
                out_specs=out_specs,
            ),
            compiler_params=pltpu.CompilerParams(
                dimension_semantics=("arbitrary",), vmem_limit_bytes=32 << 20
            ),
            cost_estimate=pl.CostEstimate(
                flops=8 * count * UNITS * BLK * steps,
                bytes_accessed=steps * BLK * (2 * count + 8 * UNITS) + 16 * count * UNITS,
                transcendentals=0,
            ),
            name=name,
        )(where, *inputs, *weights)

    total = jax.ShapeDtypeStruct((count, 2 * UNITS), jnp.float32)
    totals = call(expand_near_kernel, "expand_near", 3, near_column, rows[:3], (total, total))
    out = jax.ShapeDtypeStruct((count, 2 * UNITS), jnp.bfloat16)
    return call(
        expand_far_kernel, "expand_far", 1, far_column, (*rows[3:], *totals), out
    )


def contract_kernel(own, below, above, far_low, far_high, w_own, w_below, w_above, w_far, lent, out):
    half = far_low.shape[0]
    blocks = [
        jnp.concatenate([kept[0], lent[turn * UNITS : (turn + 1) * UNITS]], axis=0)
        for turn, kept in enumerate((w_own, w_below, w_above, w_far))
    ]
    for start, far in ((0, far_low), (half, far_high)):
        span = pl.ds(start, half)
        total = jnp.dot(own[span, :], blocks[0], preferred_element_type=jnp.float32)
        total += jnp.dot(below[span, :], blocks[1], preferred_element_type=jnp.float32)
        total += jnp.dot(above[span, :], blocks[2], preferred_element_type=jnp.float32)
        total += jnp.dot(far[...], blocks[3], preferred_element_type=jnp.float32)
        out[span, :] = total.astype(jnp.bfloat16)


def contract(acts, kept, lent):
    count = acts[0].shape[0]
    return pl.pallas_call(
        contract_kernel,
        out_shape=jax.ShapeDtypeStruct((count, BLK), jnp.bfloat16),
        compiler_params=pltpu.CompilerParams(vmem_limit_bytes=32 << 20),
        cost_estimate=pl.CostEstimate(
            flops=2 * count * FF * BLK,
            bytes_accessed=2 * (count * FF + FF * BLK + count * BLK),
            transcendentals=0,
        ),
        name="contract",
    )(*acts, *kept, lent)


def per_device(
    residual,
    queries,
    key_cache,
    value_cache,
    new_keys,
    new_values,
    cache_len,
    norm_gain,
    expert_ids,
    gate_scores,
    gate_weight,
    up_weight,
    down_weight,
):
    groups = lax.axis_size("rep")
    rows = groups * PLACES
    me = lax.axis_index("exp")
    side, place = me // 4, me % 4

    routing = jnp.concatenate([expert_ids, gate_scores], axis=-1).reshape(1, LOCAL, 2 * TOPK)
    routing = exchange(jnp.broadcast_to(routing, (N_EXP, LOCAL, 2 * TOPK)), "exp")
    routing = jnp.broadcast_to(routing[:, None], (N_EXP, 2, LOCAL, 2 * TOPK))
    routing = routing.reshape(KEYS, 2 * TOPK)

    half = UNITS // 2
    lent_gate_low = across(lax.dynamic_slice(gate_weight, (1 - side, 0, 0), (1, half, D))[0])

    hidden, normed = [], []
    for step in range(STEPS):
        attention = attend_rows(
            queries[step], key_cache, value_cache, new_keys, new_values, cache_len, step
        )
        hidden.append(residual[step].astype(jnp.float32) + attention)
        normed.append(norm_rows(hidden[-1], norm_gain))
    normed = jnp.stack(normed).reshape(LOCAL, 4, 2, HALF).transpose(1, 2, 0, 3)
    normed = jnp.broadcast_to(
        normed.reshape(1, 4, 2 * LOCAL, HALF), (2, 4, 2 * LOCAL, HALF)
    ).reshape(N_EXP, 2 * LOCAL, HALF)
    normed, lent_gate_low, gate_late, down_late = lax.optimization_barrier(
        (normed, lent_gate_low, gate_weight, down_weight)
    )
    tokens = exchange(normed, "exp").reshape(KEYS, HALF)

    def quarter(step):
        start = (place + step) % 4 * BLK
        return jnp.concatenate(
            [
                lax.dynamic_slice(down_late, (expert, 0, start), (1, UNITS, BLK))
                for expert in (side, 1 - side)
            ]
        )

    kept = [quarter(0)] + [shift(quarter(step), step) for step in (1, -1, 2)]
    lent_gate_high = across(lax.dynamic_slice(gate_late, (1 - side, half, 0), (1, half, D))[0])

    table, combine = routing_tables(routing[:, :TOPK], routing[:, TOPK:], side, groups)
    outbound = lax.dot_general(
        table, tokens, (((0,), (0,)), ((), ())), preferred_element_type=jnp.float32
    ).astype(jnp.bfloat16)

    outbound, up_late = lax.optimization_barrier((outbound, up_weight))
    inbound = exchange(outbound.reshape(groups, WIRE, HALF), "rep")
    lent_up = across(lax.dynamic_index_in_dim(up_late, 1 - side, 0, keepdims=False))
    inbound, kept, lent_gate_high = lax.optimization_barrier((inbound, kept, lent_gate_high))
    lent_down = across(jnp.concatenate([block[1] for block in kept]))
    slotted = inbound.reshape(groups, 2, PLACES, HALF).transpose(0, 2, 1, 3).reshape(rows, BLK)
    where = jnp.stack([side, place])
    weights = (gate_weight, up_weight, lent_gate_low, lent_gate_high, lent_up)
    activation = expand(where, ring(slotted), weights)
    partial_value = contract(ring(activation), kept, lent_down)
    partial_value = partial_value.reshape(groups, PLACES, 2, HALF).transpose(0, 2, 1, 3)
    returned = exchange(partial_value.reshape(groups, WIRE, HALF), "rep")
    weighted = jnp.dot(
        combine,
        returned.reshape(groups * WIRE, HALF).astype(jnp.float32),
        precision=lax.Precision.HIGHEST,
        preferred_element_type=jnp.float32,
    ).astype(jnp.bfloat16)
    expert_sum = exchange(weighted.reshape(N_EXP, 2 * LOCAL, HALF), "exp").astype(jnp.float32)
    expert_sum = expert_sum.reshape(2, 4, 2, LOCAL, HALF).sum(axis=0)
    expert_sum = expert_sum.transpose(2, 0, 1, 3).reshape(STEPS, SEQ, D)
    return (jnp.stack(hidden) + expert_sum).astype(jnp.bfloat16)


def solution(mesh):
    in_specs = (
        P(None, ("rep", "exp"), None),
        P(None, ("rep", "exp"), None),
        P(("rep", "exp"), None, None),
        P(("rep", "exp"), None, None),
        P(None, ("rep", "exp"), None),
        P(None, ("rep", "exp"), None),
        P(("rep", "exp")),
        P(),
        P(None, ("rep", "exp"), None),
        P(None, ("rep", "exp"), None),
        P("rep", "exp", None),
        P("rep", "exp", None),
        P("rep", "exp", None),
    )
    out_specs = P(None, ("rep", "exp"), None)
    return jax.shard_map(
        per_device, mesh=mesh, in_specs=in_specs, out_specs=out_specs, check_vma=False
    )
```

```python
import math

import numpy as np

import jax
import jax.numpy as jnp
from jax import lax
from jax.experimental import pallas as pl
from jax.experimental.pallas import tpu as pltpu
from jax.sharding import PartitionSpec as P

D = 4096
FF = 1536
HD = 128
QH = 32
KVH = 2
TOPK = 8
CAPE = 4
STEPS = 3
CACHE = 1024
N_EXP = 8
SEQ = 2
UNITS = FF // N_EXP
BLK = D // 4
HALF = BLK // 2
LOCAL = STEPS * SEQ
KEYS = N_EXP * 2 * LOCAL
PLACES = STEPS * CAPE
WIRE = 2 * PLACES


def attend_kernel(lengths, query, keys, values, fresh_keys, fresh_values, residual, gain, hidden, normed):
    seq = pl.program_id(0)
    group = QH // KVH
    count = STEPS * group
    length = lengths[seq]
    old_valid = lax.broadcasted_iota(jnp.int32, (count, CACHE), 1) < length
    step_of = lax.broadcasted_iota(jnp.int32, (count, 8), 0) // group
    new_valid = lax.broadcasted_iota(jnp.int32, (count, 8), 1) <= step_of
    for head in range(KVH):
        rows = slice(head * group, (head + 1) * group)
        lanes = slice(head * HD, (head + 1) * HD)
        heads = jnp.concatenate([query[step * SEQ + seq, rows] for step in range(STEPS)], axis=0)
        old = contract_last(heads, keys[0, :, lanes]) * (1.0 / math.sqrt(HD))
        new = contract_last(heads, fresh_keys[0, :, lanes]) * (1.0 / math.sqrt(HD))
        old = jnp.where(old_valid, old, -1e30)
        new = jnp.where(new_valid, new, -1e30)
        row_max = jnp.maximum(
            jnp.max(old, axis=-1, keepdims=True), jnp.max(new, axis=-1, keepdims=True)
        )
        old = jnp.exp(old - row_max)
        new = jnp.exp(new - row_max)
        total = jnp.sum(old, axis=-1, keepdims=True) + jnp.sum(new, axis=-1, keepdims=True)
        blended = jnp.dot(
            (old / total).astype(jnp.bfloat16),
            values[0, :, lanes],
            preferred_element_type=jnp.float32,
        ) + jnp.dot(
            (new / total).astype(jnp.bfloat16),
            fresh_values[0, :, lanes],
            preferred_element_type=jnp.float32,
        )
        for step in range(STEPS):
            token = step * SEQ + seq
            hidden[token, rows] = (
                residual[token, rows].astype(jnp.float32)
                + blended[step * group : (step + 1) * group]
            )
    for step in range(STEPS):
        token = step * SEQ + seq
        value = hidden[token]
        mean_square = jnp.sum(value * value) / D
        scale = lax.rsqrt(jnp.full((QH, HD), mean_square + 1e-06, jnp.float32))
        normed[token] = (value * scale * gain[...].astype(jnp.float32)).astype(jnp.bfloat16)


def attend(cache_len, queries, key_cache, value_cache, new_keys, new_values, residual, norm_gain):
    def fresh(array):
        return jnp.pad(array.transpose(1, 0, 2), ((0, 0), (0, 8 - STEPS), (0, 0)))

    def whole(shape):
        return pl.BlockSpec(shape, lambda seq, lengths: (0,) * len(shape))

    def one(shape):
        return pl.BlockSpec((1, *shape[1:]), lambda seq, lengths: (seq, 0, 0))

    tokens = (LOCAL, QH, HD)
    cache = (SEQ, CACHE, KVH * HD)
    extra = (SEQ, 8, KVH * HD)
    return pl.pallas_call(
        attend_kernel,
        out_shape=(
            jax.ShapeDtypeStruct(tokens, jnp.float32),
            jax.ShapeDtypeStruct(tokens, jnp.bfloat16),
        ),
        grid_spec=pltpu.PrefetchScalarGridSpec(
            num_scalar_prefetch=1,
            grid=(SEQ,),
            in_specs=[
                whole(tokens),
                one(cache),
                one(cache),
                one(extra),
                one(extra),
                whole(tokens),
                whole((QH, HD)),
            ],
            out_specs=(whole(tokens), whole(tokens)),
        ),
        compiler_params=pltpu.CompilerParams(
            dimension_semantics=("arbitrary",), vmem_limit_bytes=24 << 20
        ),
        cost_estimate=pl.CostEstimate(
            flops=4 * LOCAL * QH * HD * CACHE,
            bytes_accessed=4 * SEQ * CACHE * KVH * HD + 10 * LOCAL * D,
            transcendentals=LOCAL * QH * CACHE,
        ),
        name="attend",
    )(
        cache_len,
        queries.reshape(tokens),
        key_cache,
        value_cache,
        fresh(new_keys),
        fresh(new_values),
        residual.reshape(tokens),
        norm_gain.reshape(QH, HD),
    )


def exchange(array, axis):
    return lax.all_to_all(array, axis, split_axis=0, concat_axis=0, tiled=True)


def shift(array, step):
    pairs = [(e, e // 4 * 4 + (e + step) % 4) for e in range(N_EXP)]
    return lax.ppermute(array, "exp", pairs)


def across(array):
    return lax.ppermute(array, "exp", [(e, e ^ 4) for e in range(N_EXP)])


def ring(block):
    half = block.shape[0] // 2
    below, above = shift(block, 1), shift(block, -1)
    return block, below, above, shift(below[:half], 1), shift(above[half:], -1)


def routing_tables(chosen, scores, side, groups):
    gate_values = scores.astype(jnp.float32)
    gate_values = gate_values / jnp.sum(gate_values, axis=-1, keepdims=True)
    key = np.arange(KEYS)
    source, half, step, seq = (
        key // (2 * LOCAL),
        key // LOCAL % 2,
        key % LOCAL // SEQ,
        key % SEQ,
    )
    order = source * SEQ + seq
    earlier = (
        (step[:, None] == step[None, :])
        & (half[:, None] == half[None, :])
        & (order[None, :] < order[:, None])
    )
    experts = 2 * lax.broadcasted_iota(jnp.int32, (1, 1, groups), 2) + side
    hits = (chosen[:, :, None] == experts).astype(jnp.float32)
    named = jnp.sum(hits, axis=1)
    weights = jnp.sum(hits * gate_values[:, :, None], axis=1)
    rank = jnp.dot(jnp.asarray(earlier, jnp.float32), named, preferred_element_type=jnp.float32)
    rank = jnp.where(named > 0, rank, -1.0)
    place = np.arange(WIRE)
    wanted = np.where(
        (half[:, None] == place[None, :] // PLACES)
        & (step[:, None] == place[None, :] % PLACES // CAPE),
        place[None, :] % CAPE,
        -2,
    ).astype(np.float32)
    table = (rank[:, :, None] == wanted[:, None, :]).astype(jnp.float32)
    combine = (table * weights[:, :, None]).reshape(KEYS, groups * WIRE)
    return table.astype(jnp.bfloat16).reshape(KEYS, groups * WIRE), combine


def contract_last(left, right):
    return lax.dot_general(
        left, right, (((1,), (1,)), ((), ())), preferred_element_type=jnp.float32
    )


def expand_near_kernel(
    where,
    own_rows,
    below_rows,
    above_rows,
    own_gate,
    own_up,
    lent_gate_low,
    lent_gate_high,
    lent_up,
    gate_total,
    up_total,
):
    turn = pl.program_id(0)
    gate_block = jnp.concatenate([own_gate[0], lent_gate_low[...], lent_gate_high[...]], axis=0)
    up_block = jnp.concatenate([own_up[0], lent_up[...]], axis=0)

    @pl.when(turn == 0)
    def _():
        gate_total[...] = contract_last(own_rows[...], gate_block)
        up_total[...] = contract_last(own_rows[...], up_block)

    @pl.when(turn == 1)
    def _():
        gate_total[...] += contract_last(below_rows[...], gate_block)
        up_total[...] += contract_last(below_rows[...], up_block)

    @pl.when(turn == 2)
    def _():
        gate_total[...] += contract_last(above_rows[...], gate_block)
        up_total[...] += contract_last(above_rows[...], up_block)


def expand_far_kernel(
    where,
    far_low,
    far_high,
    gate_total,
    up_total,
    own_gate,
    own_up,
    lent_gate_low,
    lent_gate_high,
    lent_up,
    out,
):
    gate_block = jnp.concatenate([own_gate[0], lent_gate_low[...], lent_gate_high[...]], axis=0)
    up_block = jnp.concatenate([own_up[0], lent_up[...]], axis=0)
    half = far_low.shape[0]
    for start, rows in ((0, far_low), (half, far_high)):
        span = pl.ds(start, half)
        gate = gate_total[span, :] + contract_last(rows[...], gate_block)
        up = up_total[span, :] + contract_last(rows[...], up_block)
        out[span, :] = (gate / (1.0 + jnp.exp(-gate)) * up).astype(jnp.bfloat16)


def expand(where, rows, weights):
    count = rows[0].shape[0]

    def near_column(turn, where):
        return (where[1] + jnp.where(turn == 1, 3, jnp.where(turn == 2, 1, 0))) % 4

    def far_column(turn, where):
        return (where[1] + 2) % 4

    def whole(shape):
        return pl.BlockSpec(shape, lambda turn, where: (0, 0))

    def call(kernel, name, steps, column, inputs, out_shape):
        own = pl.BlockSpec((1, UNITS, BLK), lambda turn, where: (where[0], 0, column(turn, where)))
        lent = pl.BlockSpec((UNITS, BLK), lambda turn, where: (0, column(turn, where)))
        parts = [
            pl.BlockSpec((array.shape[0], BLK), lambda turn, where: (0, column(turn, where)))
            for array in weights[2:4]
        ]
        outs = jax.tree.leaves(out_shape)
        out_specs = jax.tree.unflatten(
            jax.tree.structure(out_shape), [whole(leaf.shape) for leaf in outs]
        )
        return pl.pallas_call(
            kernel,
            out_shape=out_shape,
            grid_spec=pltpu.PrefetchScalarGridSpec(
                num_scalar_prefetch=1,
                grid=(steps,),
                in_specs=[whole(array.shape) for array in inputs] + [own, own, *parts, lent],
                out_specs=out_specs,
            ),
            compiler_params=pltpu.CompilerParams(
                dimension_semantics=("arbitrary",), vmem_limit_bytes=32 << 20
            ),
            cost_estimate=pl.CostEstimate(
                flops=8 * count * UNITS * BLK * steps,
                bytes_accessed=steps * BLK * (2 * count + 8 * UNITS) + 16 * count * UNITS,
                transcendentals=0,
            ),
            name=name,
        )(where, *inputs, *weights)

    total = jax.ShapeDtypeStruct((count, 2 * UNITS), jnp.float32)
    totals = call(expand_near_kernel, "expand_near", 3, near_column, rows[:3], (total, total))
    out = jax.ShapeDtypeStruct((count, 2 * UNITS), jnp.bfloat16)
    return call(
        expand_far_kernel, "expand_far", 1, far_column, (*rows[3:], *totals), out
    )


def contract_kernel(own, below, above, far_low, far_high, w_own, w_below, w_above, w_far, lent, out):
    half = far_low.shape[0]
    blocks = [
        jnp.concatenate([kept[0], lent[turn * UNITS : (turn + 1) * UNITS]], axis=0)
        for turn, kept in enumerate((w_own, w_below, w_above, w_far))
    ]
    for start, far in ((0, far_low), (half, far_high)):
        span = pl.ds(start, half)
        total = jnp.dot(own[span, :], blocks[0], preferred_element_type=jnp.float32)
        total += jnp.dot(below[span, :], blocks[1], preferred_element_type=jnp.float32)
        total += jnp.dot(above[span, :], blocks[2], preferred_element_type=jnp.float32)
        total += jnp.dot(far[...], blocks[3], preferred_element_type=jnp.float32)
        out[span, :] = total.astype(jnp.bfloat16)


def contract(acts, kept, lent):
    count = acts[0].shape[0]
    return pl.pallas_call(
        contract_kernel,
        out_shape=jax.ShapeDtypeStruct((count, BLK), jnp.bfloat16),
        compiler_params=pltpu.CompilerParams(vmem_limit_bytes=32 << 20),
        cost_estimate=pl.CostEstimate(
            flops=2 * count * FF * BLK,
            bytes_accessed=2 * (count * FF + FF * BLK + count * BLK),
            transcendentals=0,
        ),
        name="contract",
    )(*acts, *kept, lent)


def per_device(
    residual,
    queries,
    key_cache,
    value_cache,
    new_keys,
    new_values,
    cache_len,
    norm_gain,
    expert_ids,
    gate_scores,
    gate_weight,
    up_weight,
    down_weight,
):
    groups = lax.axis_size("rep")
    rows = groups * PLACES
    me = lax.axis_index("exp")
    side, place = me // 4, me % 4

    routing = jnp.concatenate([expert_ids, gate_scores], axis=-1).reshape(1, LOCAL, 2 * TOPK)
    routing = exchange(jnp.broadcast_to(routing, (N_EXP, LOCAL, 2 * TOPK)), "exp")
    routing = jnp.broadcast_to(routing[:, None], (N_EXP, 2, LOCAL, 2 * TOPK))
    routing = routing.reshape(KEYS, 2 * TOPK)

    early = 2 * UNITS // 3
    lent_gate_low = across(lax.dynamic_slice(gate_weight, (1 - side, 0, 0), (1, early, D))[0])

    def quarter(weight, step):
        start = (place + step) % 4 * BLK
        return jnp.concatenate(
            [
                lax.dynamic_slice(weight, (expert, 0, start), (1, UNITS, BLK))
                for expert in (side, 1 - side)
            ]
        )

    kept_near = [shift(quarter(down_weight, step), step) for step in (1, -1)]

    hidden, normed = attend(
        cache_len, queries, key_cache, value_cache, new_keys, new_values, residual, norm_gain
    )
    normed = normed.reshape(LOCAL, 4, 2, HALF).transpose(1, 2, 0, 3)
    normed = jnp.broadcast_to(
        normed.reshape(1, 4, 2 * LOCAL, HALF), (2, 4, 2 * LOCAL, HALF)
    ).reshape(N_EXP, 2 * LOCAL, HALF)
    normed, lent_gate_low, kept_near = lax.optimization_barrier((normed, lent_gate_low, kept_near))
    tokens = exchange(normed, "exp").reshape(KEYS, HALF)
    table, combine = routing_tables(routing[:, :TOPK], routing[:, TOPK:], side, groups)
    outbound = lax.dot_general(
        table, tokens, (((0,), (0,)), ((), ())), preferred_element_type=jnp.float32
    ).astype(jnp.bfloat16)

    outbound, gate_late, up_late, down_late = lax.optimization_barrier(
        (outbound, gate_weight, up_weight, down_weight)
    )
    inbound = exchange(outbound.reshape(groups, WIRE, HALF), "rep")
    kept_far = shift(quarter(down_late, 2), 2)
    lent_gate_high = across(
        lax.dynamic_slice(gate_late, (1 - side, early, 0), (1, UNITS - early, D))[0]
    )
    lent_up = across(lax.dynamic_index_in_dim(up_late, 1 - side, 0, keepdims=False))
    inbound, kept_far, lent_gate_high = lax.optimization_barrier(
        (inbound, kept_far, lent_gate_high)
    )
    kept = [quarter(down_late, 0), *kept_near, kept_far]
    lent_down = across(jnp.concatenate([block[1] for block in kept]))
    slotted = inbound.reshape(groups, 2, PLACES, HALF).transpose(0, 2, 1, 3).reshape(rows, BLK)
    where = jnp.stack([side, place])
    weights = (gate_weight, up_weight, lent_gate_low, lent_gate_high, lent_up)
    activation = expand(where, ring(slotted), weights)
    partial_value = contract(ring(activation), kept, lent_down)
    partial_value = partial_value.reshape(groups, PLACES, 2, HALF).transpose(0, 2, 1, 3)
    returned = exchange(partial_value.reshape(groups, WIRE, HALF), "rep")
    weighted = jnp.dot(
        combine,
        returned.reshape(groups * WIRE, HALF).astype(jnp.float32),
        precision=lax.Precision.HIGHEST,
        preferred_element_type=jnp.float32,
    ).astype(jnp.bfloat16)
    expert_sum = exchange(weighted.reshape(N_EXP, 2 * LOCAL, HALF), "exp").astype(jnp.float32)
    expert_sum = expert_sum.reshape(2, 4, 2, LOCAL, HALF).sum(axis=0)
    expert_sum = expert_sum.transpose(2, 0, 1, 3).reshape(STEPS, SEQ, D)
    return (hidden.reshape(STEPS, SEQ, D) + expert_sum).astype(jnp.bfloat16)


def solution(mesh):
    in_specs = (
        P(None, ("rep", "exp"), None),
        P(None, ("rep", "exp"), None),
        P(("rep", "exp"), None, None),
        P(("rep", "exp"), None, None),
        P(None, ("rep", "exp"), None),
        P(None, ("rep", "exp"), None),
        P(("rep", "exp")),
        P(),
        P(None, ("rep", "exp"), None),
        P(None, ("rep", "exp"), None),
        P("rep", "exp", None),
        P("rep", "exp", None),
        P("rep", "exp", None),
    )
    out_specs = P(None, ("rep", "exp"), None)
    return jax.shard_map(
        per_device, mesh=mesh, in_specs=in_specs, out_specs=out_specs, check_vma=False
    )
```

```python
import math

import numpy as np

import jax
import jax.numpy as jnp
from jax import lax
from jax.experimental import pallas as pl
from jax.experimental.pallas import tpu as pltpu
from jax.sharding import PartitionSpec as P

D = 4096
FF = 1536
HD = 128
QH = 32
KVH = 2
TOPK = 8
CAPE = 4
STEPS = 3
CACHE = 1024
N_EXP = 8
SEQ = 2
UNITS = FF // N_EXP
BLK = D // 4
HALF = BLK // 2
LOCAL = STEPS * SEQ
KEYS = N_EXP * 2 * LOCAL
PLACES = STEPS * CAPE
WIRE = 2 * PLACES


def attend_kernel(lengths, query, keys, values, fresh_keys, fresh_values, residual, gain, hidden, normed):
    seq = pl.program_id(0)
    group = QH // KVH
    count = STEPS * group
    length = lengths[seq]
    old_valid = lax.broadcasted_iota(jnp.int32, (count, CACHE), 1) < length
    step_of = lax.broadcasted_iota(jnp.int32, (count, 8), 0) // group
    new_valid = lax.broadcasted_iota(jnp.int32, (count, 8), 1) <= step_of
    for head in range(KVH):
        rows = slice(head * group, (head + 1) * group)
        lanes = slice(head * HD, (head + 1) * HD)
        heads = jnp.concatenate([query[step * SEQ + seq, rows] for step in range(STEPS)], axis=0)
        old = contract_last(heads, keys[0, :, lanes]) * (1.0 / math.sqrt(HD))
        new = contract_last(heads, fresh_keys[0, :, lanes]) * (1.0 / math.sqrt(HD))
        old = jnp.where(old_valid, old, -1e30)
        new = jnp.where(new_valid, new, -1e30)
        row_max = jnp.maximum(
            jnp.max(old, axis=-1, keepdims=True), jnp.max(new, axis=-1, keepdims=True)
        )
        old = jnp.exp(old - row_max)
        new = jnp.exp(new - row_max)
        total = jnp.sum(old, axis=-1, keepdims=True) + jnp.sum(new, axis=-1, keepdims=True)
        blended = jnp.dot(
            (old / total).astype(jnp.bfloat16),
            values[0, :, lanes],
            preferred_element_type=jnp.float32,
        ) + jnp.dot(
            (new / total).astype(jnp.bfloat16),
            fresh_values[0, :, lanes],
            preferred_element_type=jnp.float32,
        )
        for step in range(STEPS):
            token = step * SEQ + seq
            hidden[token, rows] = (
                residual[token, rows].astype(jnp.float32)
                + blended[step * group : (step + 1) * group]
            )
    for step in range(STEPS):
        token = step * SEQ + seq
        value = hidden[token]
        mean_square = jnp.sum(value * value) / D
        scale = lax.rsqrt(jnp.full((QH, HD), mean_square + 1e-06, jnp.float32))
        normed[token] = (value * scale * gain[...].astype(jnp.float32)).astype(jnp.bfloat16)


def attend(cache_len, queries, key_cache, value_cache, new_keys, new_values, residual, norm_gain):
    def fresh(array):
        return jnp.pad(array.transpose(1, 0, 2), ((0, 0), (0, 8 - STEPS), (0, 0)))

    def whole(shape):
        return pl.BlockSpec(shape, lambda seq, lengths: (0,) * len(shape))

    def one(shape):
        return pl.BlockSpec((1, *shape[1:]), lambda seq, lengths: (seq, 0, 0))

    tokens = (LOCAL, QH, HD)
    cache = (SEQ, CACHE, KVH * HD)
    extra = (SEQ, 8, KVH * HD)
    return pl.pallas_call(
        attend_kernel,
        out_shape=(
            jax.ShapeDtypeStruct(tokens, jnp.float32),
            jax.ShapeDtypeStruct(tokens, jnp.bfloat16),
        ),
        grid_spec=pltpu.PrefetchScalarGridSpec(
            num_scalar_prefetch=1,
            grid=(SEQ,),
            in_specs=[
                whole(tokens),
                one(cache),
                one(cache),
                one(extra),
                one(extra),
                whole(tokens),
                whole((QH, HD)),
            ],
            out_specs=(whole(tokens), whole(tokens)),
        ),
        compiler_params=pltpu.CompilerParams(
            dimension_semantics=("arbitrary",), vmem_limit_bytes=24 << 20
        ),
        cost_estimate=pl.CostEstimate(
            flops=4 * LOCAL * QH * HD * CACHE,
            bytes_accessed=4 * SEQ * CACHE * KVH * HD + 10 * LOCAL * D,
            transcendentals=LOCAL * QH * CACHE,
        ),
        name="attend",
    )(
        cache_len,
        queries.reshape(tokens),
        key_cache,
        value_cache,
        fresh(new_keys),
        fresh(new_values),
        residual.reshape(tokens),
        norm_gain.reshape(QH, HD),
    )


def exchange(array, axis):
    return lax.all_to_all(array, axis, split_axis=0, concat_axis=0, tiled=True)


def shift(array, step):
    pairs = [(e, e // 4 * 4 + (e + step) % 4) for e in range(N_EXP)]
    return lax.ppermute(array, "exp", pairs)


def across(array):
    return lax.ppermute(array, "exp", [(e, e ^ 4) for e in range(N_EXP)])


def ring(block):
    half = block.shape[0] // 2
    below, above = shift(block, 1), shift(block, -1)
    return block, below, above, shift(below[:half], 1), shift(above[half:], -1)


def routing_tables(chosen, scores, side, groups):
    gate_values = scores.astype(jnp.float32)
    gate_values = gate_values / jnp.sum(gate_values, axis=-1, keepdims=True)
    key = np.arange(KEYS)
    source, half, step, seq = (
        key // (2 * LOCAL),
        key // LOCAL % 2,
        key % LOCAL // SEQ,
        key % SEQ,
    )
    order = source * SEQ + seq
    earlier = (
        (step[:, None] == step[None, :])
        & (half[:, None] == half[None, :])
        & (order[None, :] < order[:, None])
    )
    experts = 2 * lax.broadcasted_iota(jnp.int32, (1, 1, groups), 2) + side
    hits = (chosen[:, :, None] == experts).astype(jnp.float32)
    named = jnp.sum(hits, axis=1)
    weights = jnp.sum(hits * gate_values[:, :, None], axis=1)
    rank = jnp.dot(jnp.asarray(earlier, jnp.float32), named, preferred_element_type=jnp.float32)
    rank = jnp.where(named > 0, rank, -1.0)
    place = np.arange(WIRE)
    wanted = np.where(
        (half[:, None] == place[None, :] // PLACES)
        & (step[:, None] == place[None, :] % PLACES // CAPE),
        place[None, :] % CAPE,
        -2,
    ).astype(np.float32)
    table = (rank[:, :, None] == wanted[:, None, :]).astype(jnp.float32)
    combine = (table * weights[:, :, None]).reshape(KEYS, groups * WIRE)
    return table.astype(jnp.bfloat16).reshape(KEYS, groups * WIRE), combine


def contract_last(left, right):
    return lax.dot_general(
        left, right, (((1,), (1,)), ((), ())), preferred_element_type=jnp.float32
    )


def expand_near_kernel(
    where,
    own_rows,
    below_rows,
    above_rows,
    own_gate,
    own_up,
    lent_gate_low,
    lent_gate_high,
    lent_up,
    gate_total,
    up_total,
):
    turn = pl.program_id(0)
    gate_block = jnp.concatenate([own_gate[0], lent_gate_low[...], lent_gate_high[...]], axis=0)
    up_block = jnp.concatenate([own_up[0], lent_up[...]], axis=0)

    @pl.when(turn == 0)
    def _():
        gate_total[...] = contract_last(own_rows[...], gate_block)
        up_total[...] = contract_last(own_rows[...], up_block)

    @pl.when(turn == 1)
    def _():
        gate_total[...] += contract_last(below_rows[...], gate_block)
        up_total[...] += contract_last(below_rows[...], up_block)

    @pl.when(turn == 2)
    def _():
        gate_total[...] += contract_last(above_rows[...], gate_block)
        up_total[...] += contract_last(above_rows[...], up_block)


def expand_far_kernel(
    where,
    far_low,
    far_high,
    gate_total,
    up_total,
    own_gate,
    own_up,
    lent_gate_low,
    lent_gate_high,
    lent_up,
    out,
):
    gate_block = jnp.concatenate([own_gate[0], lent_gate_low[...], lent_gate_high[...]], axis=0)
    up_block = jnp.concatenate([own_up[0], lent_up[...]], axis=0)
    half = far_low.shape[0]
    for start, rows in ((0, far_low), (half, far_high)):
        span = pl.ds(start, half)
        gate = gate_total[span, :] + contract_last(rows[...], gate_block)
        up = up_total[span, :] + contract_last(rows[...], up_block)
        out[span, :] = (gate / (1.0 + jnp.exp(-gate)) * up).astype(jnp.bfloat16)


def expand(where, rows, weights):
    count = rows[0].shape[0]

    def near_column(turn, where):
        return (where[1] + jnp.where(turn == 1, 3, jnp.where(turn == 2, 1, 0))) % 4

    def far_column(turn, where):
        return (where[1] + 2) % 4

    def whole(shape):
        return pl.BlockSpec(shape, lambda turn, where: (0, 0))

    def call(kernel, name, steps, column, inputs, out_shape):
        own = pl.BlockSpec((1, UNITS, BLK), lambda turn, where: (where[0], 0, column(turn, where)))
        lent = pl.BlockSpec((UNITS, BLK), lambda turn, where: (0, column(turn, where)))
        parts = [
            pl.BlockSpec((array.shape[0], BLK), lambda turn, where: (0, column(turn, where)))
            for array in weights[2:4]
        ]
        outs = jax.tree.leaves(out_shape)
        out_specs = jax.tree.unflatten(
            jax.tree.structure(out_shape), [whole(leaf.shape) for leaf in outs]
        )
        return pl.pallas_call(
            kernel,
            out_shape=out_shape,
            grid_spec=pltpu.PrefetchScalarGridSpec(
                num_scalar_prefetch=1,
                grid=(steps,),
                in_specs=[whole(array.shape) for array in inputs] + [own, own, *parts, lent],
                out_specs=out_specs,
            ),
            compiler_params=pltpu.CompilerParams(
                dimension_semantics=("arbitrary",), vmem_limit_bytes=32 << 20
            ),
            cost_estimate=pl.CostEstimate(
                flops=8 * count * UNITS * BLK * steps,
                bytes_accessed=steps * BLK * (2 * count + 8 * UNITS) + 16 * count * UNITS,
                transcendentals=0,
            ),
            name=name,
        )(where, *inputs, *weights)

    total = jax.ShapeDtypeStruct((count, 2 * UNITS), jnp.float32)
    totals = call(expand_near_kernel, "expand_near", 3, near_column, rows[:3], (total, total))
    out = jax.ShapeDtypeStruct((count, 2 * UNITS), jnp.bfloat16)
    return call(
        expand_far_kernel, "expand_far", 1, far_column, (*rows[3:], *totals), out
    )


def contract_kernel(own, below, above, far_low, far_high, w_own, w_below, w_above, w_far, lent, out):
    half = far_low.shape[0]
    blocks = [
        jnp.concatenate([kept[0], lent[turn * UNITS : (turn + 1) * UNITS]], axis=0)
        for turn, kept in enumerate((w_own, w_below, w_above, w_far))
    ]
    for start, far in ((0, far_low), (half, far_high)):
        span = pl.ds(start, half)
        total = jnp.dot(own[span, :], blocks[0], preferred_element_type=jnp.float32)
        total += jnp.dot(below[span, :], blocks[1], preferred_element_type=jnp.float32)
        total += jnp.dot(above[span, :], blocks[2], preferred_element_type=jnp.float32)
        total += jnp.dot(far[...], blocks[3], preferred_element_type=jnp.float32)
        out[span, :] = total.astype(jnp.bfloat16)


def contract(acts, kept, lent):
    count = acts[0].shape[0]
    return pl.pallas_call(
        contract_kernel,
        out_shape=jax.ShapeDtypeStruct((count, BLK), jnp.bfloat16),
        compiler_params=pltpu.CompilerParams(vmem_limit_bytes=32 << 20),
        cost_estimate=pl.CostEstimate(
            flops=2 * count * FF * BLK,
            bytes_accessed=2 * (count * FF + FF * BLK + count * BLK),
            transcendentals=0,
        ),
        name="contract",
    )(*acts, *kept, lent)


def per_device(
    residual,
    queries,
    key_cache,
    value_cache,
    new_keys,
    new_values,
    cache_len,
    norm_gain,
    expert_ids,
    gate_scores,
    gate_weight,
    up_weight,
    down_weight,
):
    groups = lax.axis_size("rep")
    rows = groups * PLACES
    me = lax.axis_index("exp")
    side, place = me // 4, me % 4

    routing = jnp.concatenate([expert_ids, gate_scores], axis=-1).reshape(1, LOCAL, 2 * TOPK)
    routing = exchange(jnp.broadcast_to(routing, (N_EXP, LOCAL, 2 * TOPK)), "exp")
    routing = jnp.broadcast_to(routing[:, None], (N_EXP, 2, LOCAL, 2 * TOPK))
    routing = routing.reshape(KEYS, 2 * TOPK)

    early = 3 * UNITS // 4
    lent_gate_low = across(lax.dynamic_slice(gate_weight, (1 - side, 0, 0), (1, early, D))[0])

    def quarter(weight, step):
        start = (place + step) % 4 * BLK
        return jnp.concatenate(
            [
                lax.dynamic_slice(weight, (expert, 0, start), (1, UNITS, BLK))
                for expert in (side, 1 - side)
            ]
        )

    kept_near = [shift(quarter(down_weight, step), step) for step in (1, -1)]

    hidden, normed = attend(
        cache_len, queries, key_cache, value_cache, new_keys, new_values, residual, norm_gain
    )
    normed = normed.reshape(LOCAL, 4, 2, HALF).transpose(1, 2, 0, 3)
    normed = jnp.broadcast_to(
        normed.reshape(1, 4, 2 * LOCAL, HALF), (2, 4, 2 * LOCAL, HALF)
    ).reshape(N_EXP, 2 * LOCAL, HALF)
    normed, lent_gate_low, kept_near, gate_late, up_late = lax.optimization_barrier(
        (normed, lent_gate_low, kept_near, gate_weight, up_weight)
    )
    tokens = exchange(normed, "exp").reshape(KEYS, HALF)
    table, combine = routing_tables(routing[:, :TOPK], routing[:, TOPK:], side, groups)
    outbound = lax.dot_general(
        table, tokens, (((0,), (0,)), ((), ())), preferred_element_type=jnp.float32
    ).astype(jnp.bfloat16)

    lent_gate_high = across(
        lax.dynamic_slice(gate_late, (1 - side, early, 0), (1, UNITS - early, D))[0]
    )
    lent_up = across(lax.dynamic_index_in_dim(up_late, 1 - side, 0, keepdims=False))
    outbound, lent_gate_high, down_late = lax.optimization_barrier(
        (outbound, lent_gate_high, down_weight)
    )
    inbound = exchange(outbound.reshape(groups, WIRE, HALF), "rep")
    kept_far = shift(quarter(down_late, 2), 2)
    inbound, kept_far, lent_up = lax.optimization_barrier((inbound, kept_far, lent_up))
    kept = [quarter(down_late, 0), *kept_near, kept_far]
    lent_down = across(jnp.concatenate([block[1] for block in kept]))
    slotted = inbound.reshape(groups, 2, PLACES, HALF).transpose(0, 2, 1, 3).reshape(rows, BLK)
    where = jnp.stack([side, place])
    weights = (gate_weight, up_weight, lent_gate_low, lent_gate_high, lent_up)
    activation = expand(where, ring(slotted), weights)
    partial_value = contract(ring(activation), kept, lent_down)
    partial_value = partial_value.reshape(groups, PLACES, 2, HALF).transpose(0, 2, 1, 3)
    returned = exchange(partial_value.reshape(groups, WIRE, HALF), "rep")
    weighted = jnp.dot(
        combine,
        returned.reshape(groups * WIRE, HALF).astype(jnp.float32),
        precision=lax.Precision.HIGHEST,
        preferred_element_type=jnp.float32,
    ).astype(jnp.bfloat16)
    expert_sum = exchange(weighted.reshape(N_EXP, 2 * LOCAL, HALF), "exp").astype(jnp.float32)
    expert_sum = expert_sum.reshape(2, 4, 2, LOCAL, HALF).sum(axis=0)
    expert_sum = expert_sum.transpose(2, 0, 1, 3).reshape(STEPS, SEQ, D)
    return (hidden.reshape(STEPS, SEQ, D) + expert_sum).astype(jnp.bfloat16)


def solution(mesh):
    in_specs = (
        P(None, ("rep", "exp"), None),
        P(None, ("rep", "exp"), None),
        P(("rep", "exp"), None, None),
        P(("rep", "exp"), None, None),
        P(None, ("rep", "exp"), None),
        P(None, ("rep", "exp"), None),
        P(("rep", "exp")),
        P(),
        P(None, ("rep", "exp"), None),
        P(None, ("rep", "exp"), None),
        P("rep", "exp", None),
        P("rep", "exp", None),
        P("rep", "exp", None),
    )
    out_specs = P(None, ("rep", "exp"), None)
    return jax.shard_map(
        per_device, mesh=mesh, in_specs=in_specs, out_specs=out_specs, check_vma=False
    )
```

```python
import math

import numpy as np

import jax
import jax.numpy as jnp
from jax import lax
from jax.experimental import pallas as pl
from jax.experimental.pallas import tpu as pltpu
from jax.sharding import PartitionSpec as P

D = 4096
FF = 1536
HD = 128
QH = 32
KVH = 2
TOPK = 8
CAPE = 4
STEPS = 3
CACHE = 1024
N_EXP = 8
SEQ = 2
UNITS = FF // N_EXP
BLK = D // 4
HALF = BLK // 2
LOCAL = STEPS * SEQ
KEYS = N_EXP * 2 * LOCAL
PLACES = STEPS * CAPE
WIRE = 2 * PLACES


def attend_kernel(lengths, query, keys, values, fresh_keys, fresh_values, residual, gain, hidden, normed):
    seq = pl.program_id(0)
    group = QH // KVH
    count = STEPS * group
    length = lengths[seq]
    old_valid = lax.broadcasted_iota(jnp.int32, (count, CACHE), 1) < length
    step_of = lax.broadcasted_iota(jnp.int32, (count, 8), 0) // group
    new_valid = lax.broadcasted_iota(jnp.int32, (count, 8), 1) <= step_of
    for head in range(KVH):
        rows = slice(head * group, (head + 1) * group)
        lanes = slice(head * HD, (head + 1) * HD)
        heads = jnp.concatenate([query[step * SEQ + seq, rows] for step in range(STEPS)], axis=0)
        old = contract_last(heads, keys[0, :, lanes]) * (1.0 / math.sqrt(HD))
        new = contract_last(heads, fresh_keys[0, :, lanes]) * (1.0 / math.sqrt(HD))
        old = jnp.where(old_valid, old, -1e30)
        new = jnp.where(new_valid, new, -1e30)
        row_max = jnp.maximum(
            jnp.max(old, axis=-1, keepdims=True), jnp.max(new, axis=-1, keepdims=True)
        )
        old = jnp.exp(old - row_max)
        new = jnp.exp(new - row_max)
        total = jnp.sum(old, axis=-1, keepdims=True) + jnp.sum(new, axis=-1, keepdims=True)
        blended = jnp.dot(
            (old / total).astype(jnp.bfloat16),
            values[0, :, lanes],
            preferred_element_type=jnp.float32,
        ) + jnp.dot(
            (new / total).astype(jnp.bfloat16),
            fresh_values[0, :, lanes],
            preferred_element_type=jnp.float32,
        )
        for step in range(STEPS):
            token = step * SEQ + seq
            hidden[token, rows] = (
                residual[token, rows].astype(jnp.float32)
                + blended[step * group : (step + 1) * group]
            )
    for step in range(STEPS):
        token = step * SEQ + seq
        value = hidden[token]
        mean_square = jnp.sum(value * value) / D
        scale = lax.rsqrt(jnp.full((QH, HD), mean_square + 1e-06, jnp.float32))
        normed[token] = (value * scale * gain[...].astype(jnp.float32)).astype(jnp.bfloat16)


def attend(cache_len, queries, key_cache, value_cache, new_keys, new_values, residual, norm_gain):
    def fresh(array):
        return jnp.pad(array.transpose(1, 0, 2), ((0, 0), (0, 8 - STEPS), (0, 0)))

    def whole(shape):
        return pl.BlockSpec(shape, lambda seq, lengths: (0,) * len(shape))

    def one(shape):
        return pl.BlockSpec((1, *shape[1:]), lambda seq, lengths: (seq, 0, 0))

    tokens = (LOCAL, QH, HD)
    cache = (SEQ, CACHE, KVH * HD)
    extra = (SEQ, 8, KVH * HD)
    return pl.pallas_call(
        attend_kernel,
        out_shape=(
            jax.ShapeDtypeStruct(tokens, jnp.float32),
            jax.ShapeDtypeStruct(tokens, jnp.bfloat16),
        ),
        grid_spec=pltpu.PrefetchScalarGridSpec(
            num_scalar_prefetch=1,
            grid=(SEQ,),
            in_specs=[
                whole(tokens),
                one(cache),
                one(cache),
                one(extra),
                one(extra),
                whole(tokens),
                whole((QH, HD)),
            ],
            out_specs=(whole(tokens), whole(tokens)),
        ),
        compiler_params=pltpu.CompilerParams(
            dimension_semantics=("arbitrary",), vmem_limit_bytes=24 << 20
        ),
        cost_estimate=pl.CostEstimate(
            flops=4 * LOCAL * QH * HD * CACHE,
            bytes_accessed=4 * SEQ * CACHE * KVH * HD + 10 * LOCAL * D,
            transcendentals=LOCAL * QH * CACHE,
        ),
        name="attend",
    )(
        cache_len,
        queries.reshape(tokens),
        key_cache,
        value_cache,
        fresh(new_keys),
        fresh(new_values),
        residual.reshape(tokens),
        norm_gain.reshape(QH, HD),
    )


def exchange(array, axis):
    return lax.all_to_all(array, axis, split_axis=0, concat_axis=0, tiled=True)


def shift(array, step):
    pairs = [(e, e // 4 * 4 + (e + step) % 4) for e in range(N_EXP)]
    return lax.ppermute(array, "exp", pairs)


def across(array):
    return lax.ppermute(array, "exp", [(e, e ^ 4) for e in range(N_EXP)])


def ring(block):
    half = block.shape[0] // 2
    below, above = shift(block, 1), shift(block, -1)
    return block, below, above, shift(below[:half], 1), shift(above[half:], -1)


def routing_tables(chosen, scores, side, groups):
    gate_values = scores.astype(jnp.float32)
    gate_values = gate_values / jnp.sum(gate_values, axis=-1, keepdims=True)
    key = np.arange(KEYS)
    source, half, step, seq = (
        key // (2 * LOCAL),
        key // LOCAL % 2,
        key % LOCAL // SEQ,
        key % SEQ,
    )
    order = source * SEQ + seq
    earlier = (
        (step[:, None] == step[None, :])
        & (half[:, None] == half[None, :])
        & (order[None, :] < order[:, None])
    )
    experts = 2 * lax.broadcasted_iota(jnp.int32, (1, 1, groups), 2) + side
    hits = (chosen[:, :, None] == experts).astype(jnp.float32)
    named = jnp.sum(hits, axis=1)
    weights = jnp.sum(hits * gate_values[:, :, None], axis=1)
    rank = jnp.dot(jnp.asarray(earlier, jnp.float32), named, preferred_element_type=jnp.float32)
    rank = jnp.where(named > 0, rank, -1.0)
    place = np.arange(WIRE)
    wanted = np.where(
        (half[:, None] == place[None, :] // PLACES)
        & (step[:, None] == place[None, :] % PLACES // CAPE),
        place[None, :] % CAPE,
        -2,
    ).astype(np.float32)
    table = (rank[:, :, None] == wanted[:, None, :]).astype(jnp.float32)
    combine = (table * weights[:, :, None]).reshape(KEYS, groups * WIRE)
    return table.astype(jnp.bfloat16).reshape(KEYS, groups * WIRE), combine


def contract_last(left, right):
    return lax.dot_general(
        left, right, (((1,), (1,)), ((), ())), preferred_element_type=jnp.float32
    )


def expand_near_kernel(
    where,
    own_rows,
    below_rows,
    above_rows,
    own_gate,
    own_up,
    gate_first,
    gate_second,
    gate_third,
    lent_up,
    gate_total,
    up_total,
):
    turn = pl.program_id(0)
    gate_block = jnp.concatenate(
        [own_gate[0], gate_first[...], gate_second[...], gate_third[...]], axis=0
    )
    up_block = jnp.concatenate([own_up[0], lent_up[...]], axis=0)

    @pl.when(turn == 0)
    def _():
        gate_total[...] = contract_last(own_rows[...], gate_block)
        up_total[...] = contract_last(own_rows[...], up_block)

    @pl.when(turn == 1)
    def _():
        gate_total[...] += contract_last(below_rows[...], gate_block)
        up_total[...] += contract_last(below_rows[...], up_block)

    @pl.when(turn == 2)
    def _():
        gate_total[...] += contract_last(above_rows[...], gate_block)
        up_total[...] += contract_last(above_rows[...], up_block)


def expand_far_kernel(
    where,
    far_low,
    far_high,
    gate_total,
    up_total,
    own_gate,
    own_up,
    gate_first,
    gate_second,
    gate_third,
    lent_up,
    out,
):
    gate_block = jnp.concatenate(
        [own_gate[0], gate_first[...], gate_second[...], gate_third[...]], axis=0
    )
    up_block = jnp.concatenate([own_up[0], lent_up[...]], axis=0)
    half = far_low.shape[0]
    for start, rows in ((0, far_low), (half, far_high)):
        span = pl.ds(start, half)
        gate = gate_total[span, :] + contract_last(rows[...], gate_block)
        up = up_total[span, :] + contract_last(rows[...], up_block)
        out[span, :] = (gate / (1.0 + jnp.exp(-gate)) * up).astype(jnp.bfloat16)


def expand(where, rows, weights):
    count = rows[0].shape[0]

    def near_column(turn, where):
        return (where[1] + jnp.where(turn == 1, 3, jnp.where(turn == 2, 1, 0))) % 4

    def far_column(turn, where):
        return (where[1] + 2) % 4

    def whole(shape):
        return pl.BlockSpec(shape, lambda turn, where: (0, 0))

    def call(kernel, name, steps, column, inputs, out_shape):
        own = pl.BlockSpec((1, UNITS, BLK), lambda turn, where: (where[0], 0, column(turn, where)))
        lent = pl.BlockSpec((UNITS, BLK), lambda turn, where: (0, column(turn, where)))
        parts = [
            pl.BlockSpec((array.shape[0], BLK), lambda turn, where: (0, column(turn, where)))
            for array in weights[2:5]
        ]
        outs = jax.tree.leaves(out_shape)
        out_specs = jax.tree.unflatten(
            jax.tree.structure(out_shape), [whole(leaf.shape) for leaf in outs]
        )
        return pl.pallas_call(
            kernel,
            out_shape=out_shape,
            grid_spec=pltpu.PrefetchScalarGridSpec(
                num_scalar_prefetch=1,
                grid=(steps,),
                in_specs=[whole(array.shape) for array in inputs] + [own, own, *parts, lent],
                out_specs=out_specs,
            ),
            compiler_params=pltpu.CompilerParams(
                dimension_semantics=("arbitrary",), vmem_limit_bytes=32 << 20
            ),
            cost_estimate=pl.CostEstimate(
                flops=8 * count * UNITS * BLK * steps,
                bytes_accessed=steps * BLK * (2 * count + 8 * UNITS) + 16 * count * UNITS,
                transcendentals=0,
            ),
            name=name,
        )(where, *inputs, *weights)

    total = jax.ShapeDtypeStruct((count, 2 * UNITS), jnp.float32)
    totals = call(expand_near_kernel, "expand_near", 3, near_column, rows[:3], (total, total))
    out = jax.ShapeDtypeStruct((count, 2 * UNITS), jnp.bfloat16)
    return call(
        expand_far_kernel, "expand_far", 1, far_column, (*rows[3:], *totals), out
    )


def contract_kernel(own, below, above, far_low, far_high, w_own, w_below, w_above, w_far, lent, out):
    half = far_low.shape[0]
    blocks = [
        jnp.concatenate([kept[...], lent[turn * UNITS : (turn + 1) * UNITS]], axis=0)
        for turn, kept in enumerate((w_own, w_below, w_above, w_far))
    ]
    for start, far in ((0, far_low), (half, far_high)):
        span = pl.ds(start, half)
        total = jnp.dot(own[span, :], blocks[0], preferred_element_type=jnp.float32)
        total += jnp.dot(below[span, :], blocks[1], preferred_element_type=jnp.float32)
        total += jnp.dot(above[span, :], blocks[2], preferred_element_type=jnp.float32)
        total += jnp.dot(far[...], blocks[3], preferred_element_type=jnp.float32)
        out[span, :] = total.astype(jnp.bfloat16)


def contract(acts, kept, lent):
    count = acts[0].shape[0]
    return pl.pallas_call(
        contract_kernel,
        out_shape=jax.ShapeDtypeStruct((count, BLK), jnp.bfloat16),
        compiler_params=pltpu.CompilerParams(vmem_limit_bytes=32 << 20),
        cost_estimate=pl.CostEstimate(
            flops=2 * count * FF * BLK,
            bytes_accessed=2 * (count * FF + FF * BLK + count * BLK),
            transcendentals=0,
        ),
        name="contract",
    )(*acts, *kept, lent)


def per_device(
    residual,
    queries,
    key_cache,
    value_cache,
    new_keys,
    new_values,
    cache_len,
    norm_gain,
    expert_ids,
    gate_scores,
    gate_weight,
    up_weight,
    down_weight,
):
    groups = lax.axis_size("rep")
    rows = groups * PLACES
    me = lax.axis_index("exp")
    side, place = me // 4, me % 4

    routing = jnp.concatenate([expert_ids, gate_scores], axis=-1).reshape(1, LOCAL, 2 * TOPK)
    routing = exchange(jnp.broadcast_to(routing, (N_EXP, LOCAL, 2 * TOPK)), "exp")
    routing = jnp.broadcast_to(routing[:, None], (N_EXP, 2, LOCAL, 2 * TOPK))
    routing = routing.reshape(KEYS, 2 * TOPK)

    cuts = (0, UNITS // 2, 3 * UNITS // 4, UNITS)

    def gate_part(weight, part):
        size = (1, cuts[part + 1] - cuts[part], D)
        return across(lax.dynamic_slice(weight, (1 - side, cuts[part], 0), size)[0])

    def quarter(weight, expert, step):
        start = (place + step) % 4 * BLK
        return lax.dynamic_slice(weight, (expert, 0, start), (1, UNITS, BLK))[0]

    gate_first = gate_part(gate_weight, 0)
    lent_near = [shift(quarter(down_weight, 1 - side, step), step) for step in (1, -1)]

    hidden, normed = attend(
        cache_len, queries, key_cache, value_cache, new_keys, new_values, residual, norm_gain
    )
    normed = normed.reshape(LOCAL, 4, 2, HALF).transpose(1, 2, 0, 3)
    normed = jnp.broadcast_to(
        normed.reshape(1, 4, 2 * LOCAL, HALF), (2, 4, 2 * LOCAL, HALF)
    ).reshape(N_EXP, 2 * LOCAL, HALF)
    normed, gate_first, lent_near, gate_late = lax.optimization_barrier(
        (normed, gate_first, lent_near, gate_weight)
    )
    tokens = exchange(normed, "exp").reshape(KEYS, HALF)
    table, combine = routing_tables(routing[:, :TOPK], routing[:, TOPK:], side, groups)
    outbound = lax.dot_general(
        table, tokens, (((0,), (0,)), ((), ())), preferred_element_type=jnp.float32
    ).astype(jnp.bfloat16)

    gate_second = gate_part(gate_late, 1)
    outbound, gate_second, gate_last, up_late, down_late = lax.optimization_barrier(
        (outbound, gate_second, gate_weight, up_weight, down_weight)
    )
    inbound = exchange(outbound.reshape(groups, WIRE, HALF), "rep")
    lent_far = shift(quarter(down_late, 1 - side, 2), 2)
    kept = [shift(quarter(down_late, side, step), step) for step in (1, -1, 2)]
    gate_third = gate_part(gate_last, 2)
    lent_up = across(lax.dynamic_index_in_dim(up_late, 1 - side, 0, keepdims=False))
    inbound, lent_far, kept, gate_third = lax.optimization_barrier(
        (inbound, lent_far, kept, gate_third)
    )
    kept = [quarter(down_late, side, 0), *kept]
    lent_down = across(
        jnp.concatenate([quarter(down_late, 1 - side, 0), *lent_near, lent_far])
    )
    slotted = inbound.reshape(groups, 2, PLACES, HALF).transpose(0, 2, 1, 3).reshape(rows, BLK)
    where = jnp.stack([side, place])
    weights = (gate_weight, up_weight, gate_first, gate_second, gate_third, lent_up)
    activation = expand(where, ring(slotted), weights)
    partial_value = contract(ring(activation), kept, lent_down)
    partial_value = partial_value.reshape(groups, PLACES, 2, HALF).transpose(0, 2, 1, 3)
    returned = exchange(partial_value.reshape(groups, WIRE, HALF), "rep")
    weighted = jnp.dot(
        combine,
        returned.reshape(groups * WIRE, HALF).astype(jnp.float32),
        precision=lax.Precision.HIGHEST,
        preferred_element_type=jnp.float32,
    ).astype(jnp.bfloat16)
    expert_sum = exchange(weighted.reshape(N_EXP, 2 * LOCAL, HALF), "exp").astype(jnp.float32)
    expert_sum = expert_sum.reshape(2, 4, 2, LOCAL, HALF).sum(axis=0)
    expert_sum = expert_sum.transpose(2, 0, 1, 3).reshape(STEPS, SEQ, D)
    return (hidden.reshape(STEPS, SEQ, D) + expert_sum).astype(jnp.bfloat16)


def solution(mesh):
    in_specs = (
        P(None, ("rep", "exp"), None),
        P(None, ("rep", "exp"), None),
        P(("rep", "exp"), None, None),
        P(("rep", "exp"), None, None),
        P(None, ("rep", "exp"), None),
        P(None, ("rep", "exp"), None),
        P(("rep", "exp")),
        P(),
        P(None, ("rep", "exp"), None),
        P(None, ("rep", "exp"), None),
        P("rep", "exp", None),
        P("rep", "exp", None),
        P("rep", "exp", None),
    )
    out_specs = P(None, ("rep", "exp"), None)
    return jax.shard_map(
        per_device, mesh=mesh, in_specs=in_specs, out_specs=out_specs, check_vma=False
    )
```

```python
import math

import numpy as np

import jax
import jax.numpy as jnp
from jax import lax
from jax.experimental import pallas as pl
from jax.experimental.pallas import tpu as pltpu
from jax.sharding import PartitionSpec as P

D = 4096
FF = 1536
HD = 128
QH = 32
KVH = 2
TOPK = 8
CAPE = 4
STEPS = 3
CACHE = 1024
N_EXP = 8
SEQ = 2
UNITS = FF // N_EXP
BLK = D // 4
HALF = BLK // 2
LOCAL = STEPS * SEQ
KEYS = N_EXP * 2 * LOCAL
PLACES = STEPS * CAPE
WIRE = 2 * PLACES


def attend_kernel(lengths, query, keys, values, fresh_keys, fresh_values, residual, gain, hidden, normed):
    seq = pl.program_id(0)
    group = QH // KVH
    count = STEPS * group
    length = lengths[seq]
    old_valid = lax.broadcasted_iota(jnp.int32, (count, CACHE), 1) < length
    step_of = lax.broadcasted_iota(jnp.int32, (count, 8), 0) // group
    new_valid = lax.broadcasted_iota(jnp.int32, (count, 8), 1) <= step_of
    for head in range(KVH):
        rows = slice(head * group, (head + 1) * group)
        lanes = slice(head * HD, (head + 1) * HD)
        heads = jnp.concatenate([query[step * SEQ + seq, rows] for step in range(STEPS)], axis=0)
        old = contract_last(heads, keys[0, :, lanes]) * (1.0 / math.sqrt(HD))
        new = contract_last(heads, fresh_keys[0, :, lanes]) * (1.0 / math.sqrt(HD))
        old = jnp.where(old_valid, old, -1e30)
        new = jnp.where(new_valid, new, -1e30)
        row_max = jnp.maximum(
            jnp.max(old, axis=-1, keepdims=True), jnp.max(new, axis=-1, keepdims=True)
        )
        old = jnp.exp(old - row_max)
        new = jnp.exp(new - row_max)
        total = jnp.sum(old, axis=-1, keepdims=True) + jnp.sum(new, axis=-1, keepdims=True)
        blended = jnp.dot(
            (old / total).astype(jnp.bfloat16),
            values[0, :, lanes],
            preferred_element_type=jnp.float32,
        ) + jnp.dot(
            (new / total).astype(jnp.bfloat16),
            fresh_values[0, :, lanes],
            preferred_element_type=jnp.float32,
        )
        for step in range(STEPS):
            token = step * SEQ + seq
            hidden[token, rows] = (
                residual[token, rows].astype(jnp.float32)
                + blended[step * group : (step + 1) * group]
            )
    for step in range(STEPS):
        token = step * SEQ + seq
        value = hidden[token]
        mean_square = jnp.sum(value * value) / D
        scale = lax.rsqrt(jnp.full((QH, HD), mean_square + 1e-06, jnp.float32))
        normed[token] = (value * scale * gain[...].astype(jnp.float32)).astype(jnp.bfloat16)


def attend(cache_len, queries, key_cache, value_cache, new_keys, new_values, residual, norm_gain):
    def fresh(array):
        return jnp.pad(array.transpose(1, 0, 2), ((0, 0), (0, 8 - STEPS), (0, 0)))

    def whole(shape):
        return pl.BlockSpec(shape, lambda seq, lengths: (0,) * len(shape))

    def one(shape):
        return pl.BlockSpec((1, *shape[1:]), lambda seq, lengths: (seq, 0, 0))

    tokens = (LOCAL, QH, HD)
    cache = (SEQ, CACHE, KVH * HD)
    extra = (SEQ, 8, KVH * HD)
    return pl.pallas_call(
        attend_kernel,
        out_shape=(
            jax.ShapeDtypeStruct(tokens, jnp.float32),
            jax.ShapeDtypeStruct(tokens, jnp.bfloat16),
        ),
        grid_spec=pltpu.PrefetchScalarGridSpec(
            num_scalar_prefetch=1,
            grid=(SEQ,),
            in_specs=[
                whole(tokens),
                one(cache),
                one(cache),
                one(extra),
                one(extra),
                whole(tokens),
                whole((QH, HD)),
            ],
            out_specs=(whole(tokens), whole(tokens)),
        ),
        compiler_params=pltpu.CompilerParams(
            dimension_semantics=("arbitrary",), vmem_limit_bytes=24 << 20
        ),
        cost_estimate=pl.CostEstimate(
            flops=4 * LOCAL * QH * HD * CACHE,
            bytes_accessed=4 * SEQ * CACHE * KVH * HD + 10 * LOCAL * D,
            transcendentals=LOCAL * QH * CACHE,
        ),
        name="attend",
    )(
        cache_len,
        queries.reshape(tokens),
        key_cache,
        value_cache,
        fresh(new_keys),
        fresh(new_values),
        residual.reshape(tokens),
        norm_gain.reshape(QH, HD),
    )


def exchange(array, axis):
    return lax.all_to_all(array, axis, split_axis=0, concat_axis=0, tiled=True)


def shift(array, step):
    pairs = [(e, e // 4 * 4 + (e + step) % 4) for e in range(N_EXP)]
    return lax.ppermute(array, "exp", pairs)


def across(array):
    return lax.ppermute(array, "exp", [(e, e ^ 4) for e in range(N_EXP)])


def ring(block):
    half = block.shape[0] // 2
    below, above = shift(block, 1), shift(block, -1)
    return block, below, above, shift(below[:half], 1), shift(above[half:], -1)


def routing_tables(chosen, scores, side, groups):
    gate_values = scores.astype(jnp.float32)
    gate_values = gate_values / jnp.sum(gate_values, axis=-1, keepdims=True)
    key = np.arange(KEYS)
    source, half, step, seq = (
        key // (2 * LOCAL),
        key // LOCAL % 2,
        key % LOCAL // SEQ,
        key % SEQ,
    )
    order = source * SEQ + seq
    earlier = (
        (step[:, None] == step[None, :])
        & (half[:, None] == half[None, :])
        & (order[None, :] < order[:, None])
    )
    experts = 2 * lax.broadcasted_iota(jnp.int32, (1, 1, groups), 2) + side
    hits = (chosen[:, :, None] == experts).astype(jnp.float32)
    named = jnp.sum(hits, axis=1)
    weights = jnp.sum(hits * gate_values[:, :, None], axis=1)
    rank = jnp.dot(jnp.asarray(earlier, jnp.float32), named, preferred_element_type=jnp.float32)
    rank = jnp.where(named > 0, rank, -1.0)
    place = np.arange(WIRE)
    wanted = np.where(
        (half[:, None] == place[None, :] // PLACES)
        & (step[:, None] == place[None, :] % PLACES // CAPE),
        place[None, :] % CAPE,
        -2,
    ).astype(np.float32)
    table = (rank[:, :, None] == wanted[:, None, :]).astype(jnp.float32)
    combine = (table * weights[:, :, None]).reshape(KEYS, groups * WIRE)
    return table.astype(jnp.bfloat16).reshape(KEYS, groups * WIRE), combine


def contract_last(left, right):
    return lax.dot_general(
        left, right, (((1,), (1,)), ((), ())), preferred_element_type=jnp.float32
    )


def expand_near_kernel(
    where,
    own_rows,
    below_rows,
    above_rows,
    own_gate,
    own_up,
    gate_first,
    gate_second,
    gate_third,
    lent_up,
    gate_total,
    up_total,
):
    turn = pl.program_id(0)
    gate_block = jnp.concatenate(
        [own_gate[0], gate_first[...], gate_second[...], gate_third[...]], axis=0
    )
    up_block = jnp.concatenate([own_up[0], lent_up[...]], axis=0)

    @pl.when(turn == 0)
    def _():
        gate_total[...] = contract_last(own_rows[...], gate_block)
        up_total[...] = contract_last(own_rows[...], up_block)

    @pl.when(turn == 1)
    def _():
        gate_total[...] += contract_last(below_rows[...], gate_block)
        up_total[...] += contract_last(below_rows[...], up_block)

    @pl.when(turn == 2)
    def _():
        gate_total[...] += contract_last(above_rows[...], gate_block)
        up_total[...] += contract_last(above_rows[...], up_block)


def expand_far_kernel(
    where,
    far_low,
    far_high,
    gate_total,
    up_total,
    own_gate,
    own_up,
    gate_first,
    gate_second,
    gate_third,
    lent_up,
    out,
):
    gate_block = jnp.concatenate(
        [own_gate[0], gate_first[...], gate_second[...], gate_third[...]], axis=0
    )
    up_block = jnp.concatenate([own_up[0], lent_up[...]], axis=0)
    half = far_low.shape[0]
    for start, rows in ((0, far_low), (half, far_high)):
        span = pl.ds(start, half)
        gate = gate_total[span, :] + contract_last(rows[...], gate_block)
        up = up_total[span, :] + contract_last(rows[...], up_block)
        out[span, :] = (gate / (1.0 + jnp.exp(-gate)) * up).astype(jnp.bfloat16)


def expand(where, rows, weights):
    count = rows[0].shape[0]

    def near_column(turn, where):
        return (where[1] + jnp.where(turn == 1, 3, jnp.where(turn == 2, 1, 0))) % 4

    def far_column(turn, where):
        return (where[1] + 2) % 4

    def whole(shape):
        return pl.BlockSpec(shape, lambda turn, where: (0, 0))

    def call(kernel, name, steps, column, inputs, out_shape):
        own = pl.BlockSpec((1, UNITS, BLK), lambda turn, where: (where[0], 0, column(turn, where)))
        lent = pl.BlockSpec((UNITS, BLK), lambda turn, where: (0, column(turn, where)))
        parts = [
            pl.BlockSpec((array.shape[0], BLK), lambda turn, where: (0, column(turn, where)))
            for array in weights[2:5]
        ]
        outs = jax.tree.leaves(out_shape)
        out_specs = jax.tree.unflatten(
            jax.tree.structure(out_shape), [whole(leaf.shape) for leaf in outs]
        )
        return pl.pallas_call(
            kernel,
            out_shape=out_shape,
            grid_spec=pltpu.PrefetchScalarGridSpec(
                num_scalar_prefetch=1,
                grid=(steps,),
                in_specs=[whole(array.shape) for array in inputs] + [own, own, *parts, lent],
                out_specs=out_specs,
            ),
            compiler_params=pltpu.CompilerParams(
                dimension_semantics=("arbitrary",), vmem_limit_bytes=32 << 20
            ),
            cost_estimate=pl.CostEstimate(
                flops=8 * count * UNITS * BLK * steps,
                bytes_accessed=steps * BLK * (2 * count + 8 * UNITS) + 16 * count * UNITS,
                transcendentals=0,
            ),
            name=name,
        )(where, *inputs, *weights)

    total = jax.ShapeDtypeStruct((count, 2 * UNITS), jnp.float32)
    totals = call(expand_near_kernel, "expand_near", 3, near_column, rows[:3], (total, total))
    out = jax.ShapeDtypeStruct((count, 2 * UNITS), jnp.bfloat16)
    return call(
        expand_far_kernel, "expand_far", 1, far_column, (*rows[3:], *totals), out
    )


def contract_kernel(own, below, above, far_low, far_high, w_own, w_below, w_above, w_far, lent, out):
    half = far_low.shape[0]
    blocks = [
        jnp.concatenate([kept[...], lent[turn * UNITS : (turn + 1) * UNITS]], axis=0)
        for turn, kept in enumerate((w_own, w_below, w_above, w_far))
    ]
    for start, far in ((0, far_low), (half, far_high)):
        span = pl.ds(start, half)
        total = jnp.dot(own[span, :], blocks[0], preferred_element_type=jnp.float32)
        total += jnp.dot(below[span, :], blocks[1], preferred_element_type=jnp.float32)
        total += jnp.dot(above[span, :], blocks[2], preferred_element_type=jnp.float32)
        total += jnp.dot(far[...], blocks[3], preferred_element_type=jnp.float32)
        out[span, :] = total.astype(jnp.bfloat16)


def contract(acts, kept, lent):
    count = acts[0].shape[0]
    return pl.pallas_call(
        contract_kernel,
        out_shape=jax.ShapeDtypeStruct((count, BLK), jnp.bfloat16),
        compiler_params=pltpu.CompilerParams(vmem_limit_bytes=32 << 20),
        cost_estimate=pl.CostEstimate(
            flops=2 * count * FF * BLK,
            bytes_accessed=2 * (count * FF + FF * BLK + count * BLK),
            transcendentals=0,
        ),
        name="contract",
    )(*acts, *kept, lent)


def per_device(
    residual,
    queries,
    key_cache,
    value_cache,
    new_keys,
    new_values,
    cache_len,
    norm_gain,
    expert_ids,
    gate_scores,
    gate_weight,
    up_weight,
    down_weight,
):
    groups = lax.axis_size("rep")
    rows = groups * PLACES
    me = lax.axis_index("exp")
    side, place = me // 4, me % 4

    routing = jnp.concatenate([expert_ids, gate_scores], axis=-1).reshape(1, LOCAL, 2 * TOPK)
    routing = exchange(jnp.broadcast_to(routing, (N_EXP, LOCAL, 2 * TOPK)), "exp")
    routing = jnp.broadcast_to(routing[:, None], (N_EXP, 2, LOCAL, 2 * TOPK))
    routing = routing.reshape(KEYS, 2 * TOPK)

    cuts = (0, UNITS // 3, 2 * UNITS // 3, UNITS)

    def gate_part(weight, part):
        size = (1, cuts[part + 1] - cuts[part], D)
        return across(lax.dynamic_slice(weight, (1 - side, cuts[part], 0), size)[0])

    def quarter(weight, expert, step):
        start = (place + step) % 4 * BLK
        return lax.dynamic_slice(weight, (expert, 0, start), (1, UNITS, BLK))[0]

    gate_first = gate_part(gate_weight, 0)
    lent_near = [shift(quarter(down_weight, 1 - side, step), step) for step in (1, -1)]

    hidden, normed = attend(
        cache_len, queries, key_cache, value_cache, new_keys, new_values, residual, norm_gain
    )
    normed = normed.reshape(LOCAL, 4, 2, HALF).transpose(1, 2, 0, 3)
    normed = jnp.broadcast_to(
        normed.reshape(1, 4, 2 * LOCAL, HALF), (2, 4, 2 * LOCAL, HALF)
    ).reshape(N_EXP, 2 * LOCAL, HALF)
    normed, gate_first, lent_near, gate_late, down_next = lax.optimization_barrier(
        (normed, gate_first, lent_near, gate_weight, down_weight)
    )
    tokens = exchange(normed, "exp").reshape(KEYS, HALF)
    table, combine = routing_tables(routing[:, :TOPK], routing[:, TOPK:], side, groups)
    outbound = lax.dot_general(
        table, tokens, (((0,), (0,)), ((), ())), preferred_element_type=jnp.float32
    ).astype(jnp.bfloat16)

    gate_second = gate_part(gate_late, 1)
    lent_far = shift(quarter(down_next, 1 - side, 2), 2)
    outbound, gate_second, lent_far, gate_last, up_late, down_late = lax.optimization_barrier(
        (outbound, gate_second, lent_far, gate_weight, up_weight, down_weight)
    )
    inbound = exchange(outbound.reshape(groups, WIRE, HALF), "rep")
    kept = [shift(quarter(down_late, side, step), step) for step in (1, -1, 2)]
    gate_third = gate_part(gate_last, 2)
    lent_up = across(lax.dynamic_index_in_dim(up_late, 1 - side, 0, keepdims=False))
    inbound, kept, gate_third = lax.optimization_barrier((inbound, kept, gate_third))
    kept = [quarter(down_late, side, 0), *kept]
    lent_down = across(
        jnp.concatenate([quarter(down_late, 1 - side, 0), *lent_near, lent_far])
    )
    slotted = inbound.reshape(groups, 2, PLACES, HALF).transpose(0, 2, 1, 3).reshape(rows, BLK)
    where = jnp.stack([side, place])
    weights = (gate_weight, up_weight, gate_first, gate_second, gate_third, lent_up)
    activation = expand(where, ring(slotted), weights)
    partial_value = contract(ring(activation), kept, lent_down)
    partial_value = partial_value.reshape(groups, PLACES, 2, HALF).transpose(0, 2, 1, 3)
    returned = exchange(partial_value.reshape(groups, WIRE, HALF), "rep")
    weighted = jnp.dot(
        combine,
        returned.reshape(groups * WIRE, HALF).astype(jnp.float32),
        precision=lax.Precision.HIGHEST,
        preferred_element_type=jnp.float32,
    ).astype(jnp.bfloat16)
    expert_sum = exchange(weighted.reshape(N_EXP, 2 * LOCAL, HALF), "exp").astype(jnp.float32)
    expert_sum = expert_sum.reshape(2, 4, 2, LOCAL, HALF).sum(axis=0)
    expert_sum = expert_sum.transpose(2, 0, 1, 3).reshape(STEPS, SEQ, D)
    return (hidden.reshape(STEPS, SEQ, D) + expert_sum).astype(jnp.bfloat16)


def solution(mesh):
    in_specs = (
        P(None, ("rep", "exp"), None),
        P(None, ("rep", "exp"), None),
        P(("rep", "exp"), None, None),
        P(("rep", "exp"), None, None),
        P(None, ("rep", "exp"), None),
        P(None, ("rep", "exp"), None),
        P(("rep", "exp")),
        P(),
        P(None, ("rep", "exp"), None),
        P(None, ("rep", "exp"), None),
        P("rep", "exp", None),
        P("rep", "exp", None),
        P("rep", "exp", None),
    )
    out_specs = P(None, ("rep", "exp"), None)
    return jax.shard_map(
        per_device, mesh=mesh, in_specs=in_specs, out_specs=out_specs, check_vma=False
    )
```

```python
import math

import numpy as np

import jax
import jax.numpy as jnp
from jax import lax
from jax.experimental import pallas as pl
from jax.experimental.pallas import tpu as pltpu
from jax.sharding import PartitionSpec as P

D = 4096
FF = 1536
HD = 128
QH = 32
KVH = 2
TOPK = 8
CAPE = 4
STEPS = 3
CACHE = 1024
N_EXP = 8
SEQ = 2
UNITS = FF // N_EXP
BLK = D // 4
HALF = BLK // 2
LOCAL = STEPS * SEQ
KEYS = N_EXP * 2 * LOCAL
PLACES = STEPS * CAPE
WIRE = 2 * PLACES


def attend_kernel(lengths, query, keys, values, fresh_keys, fresh_values, residual, gain, hidden, normed):
    seq = pl.program_id(0)
    group = QH // KVH
    count = STEPS * group
    length = lengths[seq]
    old_valid = lax.broadcasted_iota(jnp.int32, (count, CACHE), 1) < length
    step_of = lax.broadcasted_iota(jnp.int32, (count, 8), 0) // group
    new_valid = lax.broadcasted_iota(jnp.int32, (count, 8), 1) <= step_of
    for head in range(KVH):
        rows = slice(head * group, (head + 1) * group)
        lanes = slice(head * HD, (head + 1) * HD)
        heads = jnp.concatenate([query[step * SEQ + seq, rows] for step in range(STEPS)], axis=0)
        old = contract_last(heads, keys[0, :, lanes]) * (1.0 / math.sqrt(HD))
        new = contract_last(heads, fresh_keys[0, :, lanes]) * (1.0 / math.sqrt(HD))
        old = jnp.where(old_valid, old, -1e30)
        new = jnp.where(new_valid, new, -1e30)
        row_max = jnp.maximum(
            jnp.max(old, axis=-1, keepdims=True), jnp.max(new, axis=-1, keepdims=True)
        )
        old = jnp.exp(old - row_max)
        new = jnp.exp(new - row_max)
        total = jnp.sum(old, axis=-1, keepdims=True) + jnp.sum(new, axis=-1, keepdims=True)
        blended = jnp.dot(
            (old / total).astype(jnp.bfloat16),
            values[0, :, lanes],
            preferred_element_type=jnp.float32,
        ) + jnp.dot(
            (new / total).astype(jnp.bfloat16),
            fresh_values[0, :, lanes],
            preferred_element_type=jnp.float32,
        )
        for step in range(STEPS):
            token = step * SEQ + seq
            hidden[token, rows] = (
                residual[token, rows].astype(jnp.float32)
                + blended[step * group : (step + 1) * group]
            )
    for step in range(STEPS):
        token = step * SEQ + seq
        value = hidden[token]
        mean_square = jnp.sum(value * value) / D
        scale = lax.rsqrt(jnp.full((QH, HD), mean_square + 1e-06, jnp.float32))
        normed[token] = (value * scale * gain[...].astype(jnp.float32)).astype(jnp.bfloat16)


def attend(cache_len, queries, key_cache, value_cache, new_keys, new_values, residual, norm_gain):
    def fresh(array):
        return jnp.pad(array.transpose(1, 0, 2), ((0, 0), (0, 8 - STEPS), (0, 0)))

    def whole(shape):
        return pl.BlockSpec(shape, lambda seq, lengths: (0,) * len(shape))

    def one(shape):
        return pl.BlockSpec((1, *shape[1:]), lambda seq, lengths: (seq, 0, 0))

    tokens = (LOCAL, QH, HD)
    cache = (SEQ, CACHE, KVH * HD)
    extra = (SEQ, 8, KVH * HD)
    return pl.pallas_call(
        attend_kernel,
        out_shape=(
            jax.ShapeDtypeStruct(tokens, jnp.float32),
            jax.ShapeDtypeStruct(tokens, jnp.bfloat16),
        ),
        grid_spec=pltpu.PrefetchScalarGridSpec(
            num_scalar_prefetch=1,
            grid=(SEQ,),
            in_specs=[
                whole(tokens),
                one(cache),
                one(cache),
                one(extra),
                one(extra),
                whole(tokens),
                whole((QH, HD)),
            ],
            out_specs=(whole(tokens), whole(tokens)),
        ),
        compiler_params=pltpu.CompilerParams(
            dimension_semantics=("arbitrary",), vmem_limit_bytes=24 << 20
        ),
        cost_estimate=pl.CostEstimate(
            flops=4 * LOCAL * QH * HD * CACHE,
            bytes_accessed=4 * SEQ * CACHE * KVH * HD + 10 * LOCAL * D,
            transcendentals=LOCAL * QH * CACHE,
        ),
        name="attend",
    )(
        cache_len,
        queries.reshape(tokens),
        key_cache,
        value_cache,
        fresh(new_keys),
        fresh(new_values),
        residual.reshape(tokens),
        norm_gain.reshape(QH, HD),
    )


def exchange(array, axis):
    return lax.all_to_all(array, axis, split_axis=0, concat_axis=0, tiled=True)


def shift(array, step):
    pairs = [(e, e // 4 * 4 + (e + step) % 4) for e in range(N_EXP)]
    return lax.ppermute(array, "exp", pairs)


def across(array):
    return lax.ppermute(array, "exp", [(e, e ^ 4) for e in range(N_EXP)])


def ring(block):
    half = block.shape[0] // 2
    below, above = shift(block, 1), shift(block, -1)
    return block, below, above, shift(below[:half], 1), shift(above[half:], -1)


def routing_tables(chosen, scores, side, groups):
    gate_values = scores.astype(jnp.float32)
    gate_values = gate_values / jnp.sum(gate_values, axis=-1, keepdims=True)
    key = np.arange(KEYS)
    source, half, step, seq = (
        key // (2 * LOCAL),
        key // LOCAL % 2,
        key % LOCAL // SEQ,
        key % SEQ,
    )
    order = source * SEQ + seq
    earlier = (
        (step[:, None] == step[None, :])
        & (half[:, None] == half[None, :])
        & (order[None, :] < order[:, None])
    )
    experts = 2 * lax.broadcasted_iota(jnp.int32, (1, 1, groups), 2) + side
    hits = (chosen[:, :, None] == experts).astype(jnp.float32)
    named = jnp.sum(hits, axis=1)
    weights = jnp.sum(hits * gate_values[:, :, None], axis=1)
    rank = jnp.dot(jnp.asarray(earlier, jnp.float32), named, preferred_element_type=jnp.float32)
    rank = jnp.where(named > 0, rank, -1.0)
    place = np.arange(WIRE)
    wanted = np.where(
        (half[:, None] == place[None, :] // PLACES)
        & (step[:, None] == place[None, :] % PLACES // CAPE),
        place[None, :] % CAPE,
        -2,
    ).astype(np.float32)
    table = (rank[:, :, None] == wanted[:, None, :]).astype(jnp.float32)
    combine = (table * weights[:, :, None]).reshape(KEYS, groups * WIRE)
    return table.astype(jnp.bfloat16).reshape(KEYS, groups * WIRE), combine


def contract_last(left, right):
    return lax.dot_general(
        left, right, (((1,), (1,)), ((), ())), preferred_element_type=jnp.float32
    )


def expand_near_kernel(
    where,
    own_rows,
    below_rows,
    above_rows,
    own_gate,
    own_up,
    gate_first,
    gate_second,
    gate_third,
    lent_up,
    gate_total,
    up_total,
):
    turn = pl.program_id(0)
    gate_block = jnp.concatenate(
        [own_gate[0], gate_first[...], gate_second[...], gate_third[...]], axis=0
    )
    up_block = jnp.concatenate([own_up[0], lent_up[...]], axis=0)

    @pl.when(turn == 0)
    def _():
        gate_total[...] = contract_last(own_rows[...], gate_block)
        up_total[...] = contract_last(own_rows[...], up_block)

    @pl.when(turn == 1)
    def _():
        gate_total[...] += contract_last(below_rows[...], gate_block)
        up_total[...] += contract_last(below_rows[...], up_block)

    @pl.when(turn == 2)
    def _():
        gate_total[...] += contract_last(above_rows[...], gate_block)
        up_total[...] += contract_last(above_rows[...], up_block)


def expand_far_kernel(
    where,
    far_low,
    far_high,
    gate_total,
    up_total,
    own_gate,
    own_up,
    gate_first,
    gate_second,
    gate_third,
    lent_up,
    out,
):
    gate_block = jnp.concatenate(
        [own_gate[0], gate_first[...], gate_second[...], gate_third[...]], axis=0
    )
    up_block = jnp.concatenate([own_up[0], lent_up[...]], axis=0)
    half = far_low.shape[0]
    for start, rows in ((0, far_low), (half, far_high)):
        span = pl.ds(start, half)
        gate = gate_total[span, :] + contract_last(rows[...], gate_block)
        up = up_total[span, :] + contract_last(rows[...], up_block)
        out[span, :] = (gate / (1.0 + jnp.exp(-gate)) * up).astype(jnp.bfloat16)


def expand(where, rows, weights):
    count = rows[0].shape[0]

    def near_column(turn, where):
        return (where[1] + jnp.where(turn == 1, 3, jnp.where(turn == 2, 1, 0))) % 4

    def far_column(turn, where):
        return (where[1] + 2) % 4

    def whole(shape):
        return pl.BlockSpec(shape, lambda turn, where: (0, 0))

    def call(kernel, name, steps, column, inputs, out_shape):
        own = pl.BlockSpec((1, UNITS, BLK), lambda turn, where: (where[0], 0, column(turn, where)))
        lent = pl.BlockSpec((UNITS, BLK), lambda turn, where: (0, column(turn, where)))
        parts = [
            pl.BlockSpec((array.shape[0], BLK), lambda turn, where: (0, column(turn, where)))
            for array in weights[2:5]
        ]
        outs = jax.tree.leaves(out_shape)
        out_specs = jax.tree.unflatten(
            jax.tree.structure(out_shape), [whole(leaf.shape) for leaf in outs]
        )
        return pl.pallas_call(
            kernel,
            out_shape=out_shape,
            grid_spec=pltpu.PrefetchScalarGridSpec(
                num_scalar_prefetch=1,
                grid=(steps,),
                in_specs=[whole(array.shape) for array in inputs] + [own, own, *parts, lent],
                out_specs=out_specs,
            ),
            compiler_params=pltpu.CompilerParams(
                dimension_semantics=("arbitrary",), vmem_limit_bytes=32 << 20
            ),
            cost_estimate=pl.CostEstimate(
                flops=8 * count * UNITS * BLK * steps,
                bytes_accessed=steps * BLK * (2 * count + 8 * UNITS) + 16 * count * UNITS,
                transcendentals=0,
            ),
            name=name,
        )(where, *inputs, *weights)

    total = jax.ShapeDtypeStruct((count, 2 * UNITS), jnp.float32)
    totals = call(expand_near_kernel, "expand_near", 3, near_column, rows[:3], (total, total))
    out = jax.ShapeDtypeStruct((count, 2 * UNITS), jnp.bfloat16)
    return call(
        expand_far_kernel, "expand_far", 1, far_column, (*rows[3:], *totals), out
    )


def contract_kernel(own, below, above, far_low, far_high, w_own, w_below, w_above, w_far, lent, out):
    half = far_low.shape[0]
    blocks = [
        jnp.concatenate([kept[...], lent[turn * UNITS : (turn + 1) * UNITS]], axis=0)
        for turn, kept in enumerate((w_own, w_below, w_above, w_far))
    ]
    for start, far in ((0, far_low), (half, far_high)):
        span = pl.ds(start, half)
        total = jnp.dot(own[span, :], blocks[0], preferred_element_type=jnp.float32)
        total += jnp.dot(below[span, :], blocks[1], preferred_element_type=jnp.float32)
        total += jnp.dot(above[span, :], blocks[2], preferred_element_type=jnp.float32)
        total += jnp.dot(far[...], blocks[3], preferred_element_type=jnp.float32)
        out[span, :] = total.astype(jnp.bfloat16)


def contract(acts, kept, lent):
    count = acts[0].shape[0]
    return pl.pallas_call(
        contract_kernel,
        out_shape=jax.ShapeDtypeStruct((count, BLK), jnp.bfloat16),
        compiler_params=pltpu.CompilerParams(vmem_limit_bytes=32 << 20),
        cost_estimate=pl.CostEstimate(
            flops=2 * count * FF * BLK,
            bytes_accessed=2 * (count * FF + FF * BLK + count * BLK),
            transcendentals=0,
        ),
        name="contract",
    )(*acts, *kept, lent)


def per_device(
    residual,
    queries,
    key_cache,
    value_cache,
    new_keys,
    new_values,
    cache_len,
    norm_gain,
    expert_ids,
    gate_scores,
    gate_weight,
    up_weight,
    down_weight,
):
    groups = lax.axis_size("rep")
    rows = groups * PLACES
    me = lax.axis_index("exp")
    side, place = me // 4, me % 4

    routing = jnp.concatenate([expert_ids, gate_scores], axis=-1).reshape(1, LOCAL, 2 * TOPK)
    routing = exchange(jnp.broadcast_to(routing, (N_EXP, LOCAL, 2 * TOPK)), "exp")
    routing = jnp.broadcast_to(routing[:, None], (N_EXP, 2, LOCAL, 2 * TOPK))
    routing = routing.reshape(KEYS, 2 * TOPK)

    cuts = (0, UNITS // 3, 2 * UNITS // 3, UNITS)

    def gate_part(weight, part):
        size = (1, cuts[part + 1] - cuts[part], D)
        return across(lax.dynamic_slice(weight, (1 - side, cuts[part], 0), size)[0])

    def quarter(weight, expert, step):
        start = (place + step) % 4 * BLK
        return lax.dynamic_slice(weight, (expert, 0, start), (1, UNITS, BLK))[0]

    gate_first = gate_part(gate_weight, 0)
    lent_near = [shift(quarter(down_weight, 1 - side, step), step) for step in (1, -1)]

    hidden, normed = attend(
        cache_len, queries, key_cache, value_cache, new_keys, new_values, residual, norm_gain
    )
    normed = normed.reshape(LOCAL, 4, 2, HALF).transpose(1, 2, 0, 3)
    normed = jnp.broadcast_to(
        normed.reshape(1, 4, 2 * LOCAL, HALF), (2, 4, 2 * LOCAL, HALF)
    ).reshape(N_EXP, 2 * LOCAL, HALF)
    normed, gate_first, lent_near, up_next = lax.optimization_barrier(
        (normed, gate_first, lent_near, up_weight)
    )
    tokens = exchange(normed, "exp").reshape(KEYS, HALF)
    table, combine = routing_tables(routing[:, :TOPK], routing[:, TOPK:], side, groups)
    outbound = lax.dot_general(
        table, tokens, (((0,), (0,)), ((), ())), preferred_element_type=jnp.float32
    ).astype(jnp.bfloat16)

    lent_up = across(lax.dynamic_index_in_dim(up_next, 1 - side, 0, keepdims=False))
    outbound, gate_last, down_late = lax.optimization_barrier((outbound, gate_weight, down_weight))
    inbound = exchange(outbound.reshape(groups, WIRE, HALF), "rep")
    kept = [shift(quarter(down_late, side, step), step) for step in (1, -1, 2)]
    gate_second, gate_third = gate_part(gate_last, 1), gate_part(gate_last, 2)
    lent_far = shift(quarter(down_late, 1 - side, 2), 2)
    inbound, kept, lent_far, gate_second, gate_third, lent_up = lax.optimization_barrier(
        (inbound, kept, lent_far, gate_second, gate_third, lent_up)
    )
    kept = [quarter(down_late, side, 0), *kept]
    lent_down = across(
        jnp.concatenate([quarter(down_late, 1 - side, 0), *lent_near, lent_far])
    )
    slotted = inbound.reshape(groups, 2, PLACES, HALF).transpose(0, 2, 1, 3).reshape(rows, BLK)
    where = jnp.stack([side, place])
    weights = (gate_weight, up_weight, gate_first, gate_second, gate_third, lent_up)
    activation = expand(where, ring(slotted), weights)
    partial_value = contract(ring(activation), kept, lent_down)
    partial_value = partial_value.reshape(groups, PLACES, 2, HALF).transpose(0, 2, 1, 3)
    returned = exchange(partial_value.reshape(groups, WIRE, HALF), "rep")
    weighted = jnp.dot(
        combine,
        returned.reshape(groups * WIRE, HALF).astype(jnp.float32),
        precision=lax.Precision.HIGHEST,
        preferred_element_type=jnp.float32,
    ).astype(jnp.bfloat16)
    expert_sum = exchange(weighted.reshape(N_EXP, 2 * LOCAL, HALF), "exp").astype(jnp.float32)
    expert_sum = expert_sum.reshape(2, 4, 2, LOCAL, HALF).sum(axis=0)
    expert_sum = expert_sum.transpose(2, 0, 1, 3).reshape(STEPS, SEQ, D)
    return (hidden.reshape(STEPS, SEQ, D) + expert_sum).astype(jnp.bfloat16)


def solution(mesh):
    in_specs = (
        P(None, ("rep", "exp"), None),
        P(None, ("rep", "exp"), None),
        P(("rep", "exp"), None, None),
        P(("rep", "exp"), None, None),
        P(None, ("rep", "exp"), None),
        P(None, ("rep", "exp"), None),
        P(("rep", "exp")),
        P(),
        P(None, ("rep", "exp"), None),
        P(None, ("rep", "exp"), None),
        P("rep", "exp", None),
        P("rep", "exp", None),
        P("rep", "exp", None),
    )
    out_specs = P(None, ("rep", "exp"), None)
    return jax.shard_map(
        per_device, mesh=mesh, in_specs=in_specs, out_specs=out_specs, check_vma=False
    )
```

```python
import math

import numpy as np

import jax
import jax.numpy as jnp
from jax import lax
from jax.experimental import pallas as pl
from jax.experimental.pallas import tpu as pltpu
from jax.sharding import PartitionSpec as P

D = 4096
FF = 1536
HD = 128
QH = 32
KVH = 2
TOPK = 8
CAPE = 4
STEPS = 3
CACHE = 1024
N_EXP = 8
SEQ = 2
UNITS = FF // N_EXP
BLK = D // 4
HALF = BLK // 2
LOCAL = STEPS * SEQ
KEYS = N_EXP * 2 * LOCAL
PLACES = STEPS * CAPE
WIRE = 2 * PLACES


def attend_kernel(lengths, query, keys, values, fresh_keys, fresh_values, residual, gain, hidden, normed):
    seq = pl.program_id(0)
    group = QH // KVH
    count = STEPS * group
    length = lengths[seq]
    old_valid = lax.broadcasted_iota(jnp.int32, (count, CACHE), 1) < length
    step_of = lax.broadcasted_iota(jnp.int32, (count, 8), 0) // group
    new_valid = lax.broadcasted_iota(jnp.int32, (count, 8), 1) <= step_of
    for head in range(KVH):
        rows = slice(head * group, (head + 1) * group)
        lanes = slice(head * HD, (head + 1) * HD)
        heads = jnp.concatenate([query[step * SEQ + seq, rows] for step in range(STEPS)], axis=0)
        old = contract_last(heads, keys[0, :, lanes]) * (1.0 / math.sqrt(HD))
        new = contract_last(heads, fresh_keys[0, :, lanes]) * (1.0 / math.sqrt(HD))
        old = jnp.where(old_valid, old, -1e30)
        new = jnp.where(new_valid, new, -1e30)
        row_max = jnp.maximum(
            jnp.max(old, axis=-1, keepdims=True), jnp.max(new, axis=-1, keepdims=True)
        )
        old = jnp.exp(old - row_max)
        new = jnp.exp(new - row_max)
        total = jnp.sum(old, axis=-1, keepdims=True) + jnp.sum(new, axis=-1, keepdims=True)
        blended = jnp.dot(
            (old / total).astype(jnp.bfloat16),
            values[0, :, lanes],
            preferred_element_type=jnp.float32,
        ) + jnp.dot(
            (new / total).astype(jnp.bfloat16),
            fresh_values[0, :, lanes],
            preferred_element_type=jnp.float32,
        )
        for step in range(STEPS):
            token = step * SEQ + seq
            hidden[token, rows] = (
                residual[token, rows].astype(jnp.float32)
                + blended[step * group : (step + 1) * group]
            )
    for step in range(STEPS):
        token = step * SEQ + seq
        value = hidden[token]
        mean_square = jnp.sum(value * value) / D
        scale = lax.rsqrt(jnp.full((QH, HD), mean_square + 1e-06, jnp.float32))
        normed[token] = (value * scale * gain[...].astype(jnp.float32)).astype(jnp.bfloat16)


def attend(cache_len, queries, key_cache, value_cache, new_keys, new_values, residual, norm_gain):
    def fresh(array):
        return jnp.pad(array.transpose(1, 0, 2), ((0, 0), (0, 8 - STEPS), (0, 0)))

    def whole(shape):
        return pl.BlockSpec(shape, lambda seq, lengths: (0,) * len(shape))

    def one(shape):
        return pl.BlockSpec((1, *shape[1:]), lambda seq, lengths: (seq, 0, 0))

    tokens = (LOCAL, QH, HD)
    cache = (SEQ, CACHE, KVH * HD)
    extra = (SEQ, 8, KVH * HD)
    return pl.pallas_call(
        attend_kernel,
        out_shape=(
            jax.ShapeDtypeStruct(tokens, jnp.float32),
            jax.ShapeDtypeStruct(tokens, jnp.bfloat16),
        ),
        grid_spec=pltpu.PrefetchScalarGridSpec(
            num_scalar_prefetch=1,
            grid=(SEQ,),
            in_specs=[
                whole(tokens),
                one(cache),
                one(cache),
                one(extra),
                one(extra),
                whole(tokens),
                whole((QH, HD)),
            ],
            out_specs=(whole(tokens), whole(tokens)),
        ),
        compiler_params=pltpu.CompilerParams(
            dimension_semantics=("arbitrary",), vmem_limit_bytes=24 << 20
        ),
        cost_estimate=pl.CostEstimate(
            flops=4 * LOCAL * QH * HD * CACHE,
            bytes_accessed=4 * SEQ * CACHE * KVH * HD + 10 * LOCAL * D,
            transcendentals=LOCAL * QH * CACHE,
        ),
        name="attend",
    )(
        cache_len,
        queries.reshape(tokens),
        key_cache,
        value_cache,
        fresh(new_keys),
        fresh(new_values),
        residual.reshape(tokens),
        norm_gain.reshape(QH, HD),
    )


def exchange(array, axis):
    return lax.all_to_all(array, axis, split_axis=0, concat_axis=0, tiled=True)


def shift(array, step):
    pairs = [(e, e // 4 * 4 + (e + step) % 4) for e in range(N_EXP)]
    return lax.ppermute(array, "exp", pairs)


def across(array):
    return lax.ppermute(array, "exp", [(e, e ^ 4) for e in range(N_EXP)])


def ring(block):
    half = block.shape[0] // 2
    below, above = shift(block, 1), shift(block, -1)
    return block, below, above, shift(below[:half], 1), shift(above[half:], -1)


def routing_tables(chosen, scores, side, groups):
    gate_values = scores.astype(jnp.float32)
    gate_values = gate_values / jnp.sum(gate_values, axis=-1, keepdims=True)
    key = np.arange(KEYS)
    source, half, step, seq = (
        key // (2 * LOCAL),
        key // LOCAL % 2,
        key % LOCAL // SEQ,
        key % SEQ,
    )
    order = source * SEQ + seq
    earlier = (
        (step[:, None] == step[None, :])
        & (half[:, None] == half[None, :])
        & (order[None, :] < order[:, None])
    )
    experts = 2 * lax.broadcasted_iota(jnp.int32, (1, 1, groups), 2) + side
    hits = (chosen[:, :, None] == experts).astype(jnp.float32)
    named = jnp.sum(hits, axis=1)
    weights = jnp.sum(hits * gate_values[:, :, None], axis=1)
    rank = jnp.dot(jnp.asarray(earlier, jnp.float32), named, preferred_element_type=jnp.float32)
    rank = jnp.where(named > 0, rank, -1.0)
    place = np.arange(WIRE)
    wanted = np.where(
        (half[:, None] == place[None, :] // PLACES)
        & (step[:, None] == place[None, :] % PLACES // CAPE),
        place[None, :] % CAPE,
        -2,
    ).astype(np.float32)
    table = (rank[:, :, None] == wanted[:, None, :]).astype(jnp.float32)
    combine = (table * weights[:, :, None]).reshape(KEYS, groups * WIRE)
    return table.astype(jnp.bfloat16).reshape(KEYS, groups * WIRE), combine


def contract_last(left, right):
    return lax.dot_general(
        left, right, (((1,), (1,)), ((), ())), preferred_element_type=jnp.float32
    )


def expand_near_kernel(
    where,
    own_rows,
    below_rows,
    above_rows,
    own_gate,
    own_up,
    gate_first,
    gate_second,
    gate_third,
    lent_up,
    gate_total,
    up_total,
):
    turn = pl.program_id(0)
    gate_block = jnp.concatenate(
        [own_gate[0], gate_first[...], gate_second[...], gate_third[...]], axis=0
    )
    up_block = jnp.concatenate([own_up[0], lent_up[...]], axis=0)

    @pl.when(turn == 0)
    def _():
        gate_total[...] = contract_last(own_rows[...], gate_block)
        up_total[...] = contract_last(own_rows[...], up_block)

    @pl.when(turn == 1)
    def _():
        gate_total[...] += contract_last(below_rows[...], gate_block)
        up_total[...] += contract_last(below_rows[...], up_block)

    @pl.when(turn == 2)
    def _():
        gate_total[...] += contract_last(above_rows[...], gate_block)
        up_total[...] += contract_last(above_rows[...], up_block)


def expand_far_kernel(
    where,
    far_low,
    far_high,
    gate_total,
    up_total,
    own_gate,
    own_up,
    gate_first,
    gate_second,
    gate_third,
    lent_up,
    out,
):
    gate_block = jnp.concatenate(
        [own_gate[0], gate_first[...], gate_second[...], gate_third[...]], axis=0
    )
    up_block = jnp.concatenate([own_up[0], lent_up[...]], axis=0)
    half = far_low.shape[0]
    for start, rows in ((0, far_low), (half, far_high)):
        span = pl.ds(start, half)
        gate = gate_total[span, :] + contract_last(rows[...], gate_block)
        up = up_total[span, :] + contract_last(rows[...], up_block)
        out[span, :] = (gate / (1.0 + jnp.exp(-gate)) * up).astype(jnp.bfloat16)


def expand(where, rows, weights):
    count = rows[0].shape[0]

    def near_column(turn, where):
        return (where[1] + jnp.where(turn == 1, 3, jnp.where(turn == 2, 1, 0))) % 4

    def far_column(turn, where):
        return (where[1] + 2) % 4

    def whole(shape):
        return pl.BlockSpec(shape, lambda turn, where: (0, 0))

    def call(kernel, name, steps, column, inputs, out_shape):
        own = pl.BlockSpec((1, UNITS, BLK), lambda turn, where: (where[0], 0, column(turn, where)))
        lent = pl.BlockSpec((UNITS, BLK), lambda turn, where: (0, column(turn, where)))
        parts = [
            pl.BlockSpec((array.shape[0], BLK), lambda turn, where: (0, column(turn, where)))
            for array in weights[2:5]
        ]
        outs = jax.tree.leaves(out_shape)
        out_specs = jax.tree.unflatten(
            jax.tree.structure(out_shape), [whole(leaf.shape) for leaf in outs]
        )
        return pl.pallas_call(
            kernel,
            out_shape=out_shape,
            grid_spec=pltpu.PrefetchScalarGridSpec(
                num_scalar_prefetch=1,
                grid=(steps,),
                in_specs=[whole(array.shape) for array in inputs] + [own, own, *parts, lent],
                out_specs=out_specs,
            ),
            compiler_params=pltpu.CompilerParams(
                dimension_semantics=("arbitrary",), vmem_limit_bytes=32 << 20
            ),
            cost_estimate=pl.CostEstimate(
                flops=8 * count * UNITS * BLK * steps,
                bytes_accessed=steps * BLK * (2 * count + 8 * UNITS) + 16 * count * UNITS,
                transcendentals=0,
            ),
            name=name,
        )(where, *inputs, *weights)

    total = jax.ShapeDtypeStruct((count, 2 * UNITS), jnp.float32)
    totals = call(expand_near_kernel, "expand_near", 3, near_column, rows[:3], (total, total))
    out = jax.ShapeDtypeStruct((count, 2 * UNITS), jnp.bfloat16)
    return call(
        expand_far_kernel, "expand_far", 1, far_column, (*rows[3:], *totals), out
    )


def contract_kernel(own, below, above, far_low, far_high, w_own, w_below, w_above, w_far, lent, out):
    half = far_low.shape[0]
    blocks = [
        jnp.concatenate([kept[...], lent[turn * UNITS : (turn + 1) * UNITS]], axis=0)
        for turn, kept in enumerate((w_own, w_below, w_above, w_far))
    ]
    for start, far in ((0, far_low), (half, far_high)):
        span = pl.ds(start, half)
        total = jnp.dot(own[span, :], blocks[0], preferred_element_type=jnp.float32)
        total += jnp.dot(below[span, :], blocks[1], preferred_element_type=jnp.float32)
        total += jnp.dot(above[span, :], blocks[2], preferred_element_type=jnp.float32)
        total += jnp.dot(far[...], blocks[3], preferred_element_type=jnp.float32)
        out[span, :] = total.astype(jnp.bfloat16)


def contract(acts, kept, lent):
    count = acts[0].shape[0]
    return pl.pallas_call(
        contract_kernel,
        out_shape=jax.ShapeDtypeStruct((count, BLK), jnp.bfloat16),
        compiler_params=pltpu.CompilerParams(vmem_limit_bytes=32 << 20),
        cost_estimate=pl.CostEstimate(
            flops=2 * count * FF * BLK,
            bytes_accessed=2 * (count * FF + FF * BLK + count * BLK),
            transcendentals=0,
        ),
        name="contract",
    )(*acts, *kept, lent)


def per_device(
    residual,
    queries,
    key_cache,
    value_cache,
    new_keys,
    new_values,
    cache_len,
    norm_gain,
    expert_ids,
    gate_scores,
    gate_weight,
    up_weight,
    down_weight,
):
    groups = lax.axis_size("rep")
    rows = groups * PLACES
    me = lax.axis_index("exp")
    side, place = me // 4, me % 4

    routing = jnp.concatenate([expert_ids, gate_scores], axis=-1).reshape(1, LOCAL, 2 * TOPK)
    routing = exchange(jnp.broadcast_to(routing, (N_EXP, LOCAL, 2 * TOPK)), "exp")
    routing = jnp.broadcast_to(routing[:, None], (N_EXP, 2, LOCAL, 2 * TOPK))
    routing = routing.reshape(KEYS, 2 * TOPK)

    cuts = (0, 5 * UNITS // 12, 3 * UNITS // 4, UNITS)

    def gate_part(weight, part):
        size = (1, cuts[part + 1] - cuts[part], D)
        return across(lax.dynamic_slice(weight, (1 - side, cuts[part], 0), size)[0])

    def quarter(weight, expert, step):
        start = (place + step) % 4 * BLK
        return lax.dynamic_slice(weight, (expert, 0, start), (1, UNITS, BLK))[0]

    gate_first = gate_part(gate_weight, 0)
    lent_near = [shift(quarter(down_weight, 1 - side, step), step) for step in (1, -1)]

    hidden, normed = attend(
        cache_len, queries, key_cache, value_cache, new_keys, new_values, residual, norm_gain
    )
    normed = normed.reshape(LOCAL, 4, 2, HALF).transpose(1, 2, 0, 3)
    normed = jnp.broadcast_to(
        normed.reshape(1, 4, 2 * LOCAL, HALF), (2, 4, 2 * LOCAL, HALF)
    ).reshape(N_EXP, 2 * LOCAL, HALF)
    normed, gate_first, lent_near, gate_late, down_next = lax.optimization_barrier(
        (normed, gate_first, lent_near, gate_weight, down_weight)
    )
    tokens = exchange(normed, "exp").reshape(KEYS, HALF)
    table, combine = routing_tables(routing[:, :TOPK], routing[:, TOPK:], side, groups)
    outbound = lax.dot_general(
        table, tokens, (((0,), (0,)), ((), ())), preferred_element_type=jnp.float32
    ).astype(jnp.bfloat16)

    gate_second = gate_part(gate_late, 1)
    lent_far = shift(quarter(down_next, 1 - side, 2), 2)
    outbound, gate_second, lent_far, gate_last, up_late, down_late = lax.optimization_barrier(
        (outbound, gate_second, lent_far, gate_weight, up_weight, down_weight)
    )
    inbound = exchange(outbound.reshape(groups, WIRE, HALF), "rep")
    kept = [shift(quarter(down_late, side, step), step) for step in (1, -1, 2)]
    gate_third = gate_part(gate_last, 2)
    lent_up = across(lax.dynamic_index_in_dim(up_late, 1 - side, 0, keepdims=False))
    inbound, kept, gate_third = lax.optimization_barrier((inbound, kept, gate_third))
    kept = [quarter(down_late, side, 0), *kept]
    lent_down = across(
        jnp.concatenate([quarter(down_late, 1 - side, 0), *lent_near, lent_far])
    )
    slotted = inbound.reshape(groups, 2, PLACES, HALF).transpose(0, 2, 1, 3).reshape(rows, BLK)
    where = jnp.stack([side, place])
    weights = (gate_weight, up_weight, gate_first, gate_second, gate_third, lent_up)
    activation = expand(where, ring(slotted), weights)
    partial_value = contract(ring(activation), kept, lent_down)
    partial_value = partial_value.reshape(groups, PLACES, 2, HALF).transpose(0, 2, 1, 3)
    returned = exchange(partial_value.reshape(groups, WIRE, HALF), "rep")
    weighted = jnp.dot(
        combine,
        returned.reshape(groups * WIRE, HALF).astype(jnp.float32),
        precision=lax.Precision.HIGHEST,
        preferred_element_type=jnp.float32,
    ).astype(jnp.bfloat16)
    expert_sum = exchange(weighted.reshape(N_EXP, 2 * LOCAL, HALF), "exp").astype(jnp.float32)
    expert_sum = expert_sum.reshape(2, 4, 2, LOCAL, HALF).sum(axis=0)
    expert_sum = expert_sum.transpose(2, 0, 1, 3).reshape(STEPS, SEQ, D)
    return (hidden.reshape(STEPS, SEQ, D) + expert_sum).astype(jnp.bfloat16)


def solution(mesh):
    in_specs = (
        P(None, ("rep", "exp"), None),
        P(None, ("rep", "exp"), None),
        P(("rep", "exp"), None, None),
        P(("rep", "exp"), None, None),
        P(None, ("rep", "exp"), None),
        P(None, ("rep", "exp"), None),
        P(("rep", "exp")),
        P(),
        P(None, ("rep", "exp"), None),
        P(None, ("rep", "exp"), None),
        P("rep", "exp", None),
        P("rep", "exp", None),
        P("rep", "exp", None),
    )
    out_specs = P(None, ("rep", "exp"), None)
    return jax.shard_map(
        per_device, mesh=mesh, in_specs=in_specs, out_specs=out_specs, check_vma=False
    )
```
